32 devices in a mesh: paths: 2 (over x), hi: 16 (over z, y, core).
Axes of the slice: x: 2, y: 2, z: 4, core: 2. Of those that a mesh axis runs over, the one named last changes fastest.
Arguments:
- amplitudes: float32 [2, 2097152], P(None, ('paths', 'hi')), parts along dimension 1, may hold values from -6 to 6
- gate_matrices: bfloat16 [6, 2, 128, 128], replicated, may hold values from -0.375 to 0.375
- phase_qubits: int32 [12, 8, 2], P('paths'), parts along dimension 0, may hold values from 0 to 19
- phase_angles: float32 [12, 8], P('paths'), parts along dimension 0, may hold values from -3.140625 to 3.140625
- cut_qubits: int32 [12, 2], P('paths'), parts along dimension 0, may hold values from 0 to 19
- cut_angle: float32 [12], P('paths'), parts along dimension 0, may hold values from 0.6 to 0.97
- path_index: int32 [12], P('paths'), parts along dimension 0, may hold values from 0 to 1
Outputs:
- final_state: float32 [2, 2097152], P(None, ('paths', 'hi')), parts along dimension 1
The draws below stay inside these ranges and needn't reach their ends.
There are 2 independent parts, one for each index of `paths`. The reference program is written for one: setup_inputs(seed, part) draws one part's arguments, and reference() takes and returns one part's arrays. A program takes and returns all parts, laid end to end along the dimension named above; an argument that names none is the same for every part. Nothing has to cross between parts.
All inputs are finite; a program needn't handle non-finite values.
Results may differ from the reference program's by a relative error of at most 0.0003.
Values sent between devices are 32-bit elements; how exact they have to be, the bound alone decides.
A program may use at most 64 MiB of HBM per device.

```python
import jax
import jax.numpy as jnp
from jax import lax

LOCAL_Q = 16
GLOBAL_Q = 4
QUBITS = 20
AMPS = 1048576
GATE_DIM = 128
LAYERS = 6
PAIRS = 8
CUTS = 6


def set_ends(entries, key, least, top_value):
    dims = entries.shape
    index_at = [jax.random.randint(jax.random.fold_in(key, axis), (), 0, dims[axis]) for axis in range(len(dims))]
    entries = entries.at[tuple(index_at)].set(least)
    longest = dims.index(max(dims))
    index_at[longest] = (index_at[longest] + 1) % dims[longest]
    return entries.at[tuple(index_at)].set(top_value)


def levels(key, extent, cuts, low, high):
    def one(position, parts):
        heights = jax.random.uniform(jax.random.fold_in(jax.random.fold_in(key, 6), position), (parts,), jnp.float32, low / len(cuts), high / len(cuts))
        return jnp.repeat(jnp.exp(heights), extent[position] // parts).reshape((-1,) + (1,) * (len(extent) - position - 1))

    level = one(*cuts[0])
    for cut in cuts[1:]:
        level = level * one(*cut)
    return level


def centred(rng, shape, deviation, bound, cuts=(), held_as=jnp.bfloat16):
    drawn = jax.random.normal(rng, shape, jnp.float32) * deviation
    if len(cuts) > 0:
        drawn = levels(rng, shape, cuts, -0.22, 0.18) * drawn
    return jnp.clip(drawn, min=-bound, max=bound).astype(held_as)


def setup_inputs(seed: int = 0, part: int = 0) -> dict:
    keys = jax.random.split(jax.random.key(seed), 8)
    part_keys = jax.random.split(jax.random.fold_in(keys[7], part), 8)
    return {
        "amplitudes": centred(part_keys[0], (2, AMPS), 1.0, 6.0, ((1, 16),), jnp.float32),
        "gate_matrices": centred(keys[1], (LAYERS, 2, GATE_DIM, GATE_DIM), (2 * GATE_DIM) ** -0.5, 0.375),
        "phase_qubits": set_ends(jax.random.randint(part_keys[2], (LAYERS, PAIRS, 2), 0, QUBITS), jax.random.fold_in(part_keys[2], 1), 0, QUBITS - 1).astype(jnp.int32),
        "phase_angles": jnp.clip(jax.random.uniform(part_keys[3], (LAYERS, PAIRS), jnp.float32, -3.140625, 3.140625), -3.140625, 3.140625),
        "cut_qubits": set_ends(jax.random.randint(part_keys[4], (CUTS, 2), 0, QUBITS), jax.random.fold_in(part_keys[4], 1), 0, QUBITS - 1).astype(jnp.int32),
        "cut_angle": jnp.clip(jax.random.uniform(part_keys[5], (CUTS,), jnp.float32, 0.6, 0.97), 0.6, 0.97),
        "path_index": set_ends(jax.random.randint(part_keys[6], (CUTS,), 0, 2), jax.random.fold_in(part_keys[6], 1), 0, 1).astype(jnp.int32),
    }


def real_form(matrix):
    real_part = matrix[0].astype(jnp.float32)
    imag_part = matrix[1].astype(jnp.float32)
    upper_rows = jnp.stack((real_part, -imag_part), axis=1)
    lower_rows = jnp.stack((imag_part, real_part), axis=1)
    stacked = jnp.stack((upper_rows, lower_rows), axis=0)
    return stacked.reshape(2, 2, 64, 2, 2, 64)


def apply_gate(amps_now, matrix, target, total_bits):
    shaped = amps_now.reshape(2, 2 ** (total_bits - 1 - target), 2, 2 ** (target - 7), 2, 64)
    result = jnp.einsum("wxyzbd,zabced->waxcey", real_form(matrix), shaped,
                        precision=lax.Precision.HIGHEST)
    return result.reshape(2, -1)


def swap_bits(amps_now, low_bit, high_bit, total_bits):
    shaped = amps_now.reshape(2, 2 ** (total_bits - 1 - high_bit), 2, 2 ** (high_bit - low_bit - 1), 2, 2 ** low_bit)
    return jnp.swapaxes(shaped, 2, 4).reshape(2, -1)


def rotate(amps_now, theta):
    cosine = jnp.cos(theta)
    sine = jnp.sin(theta)
    return jnp.stack((cosine * amps_now[0] - sine * amps_now[1], sine * amps_now[0] + cosine * amps_now[1]))


def bit_of(index_all, qubit):
    return jnp.bitwise_and(jnp.right_shift(index_all, qubit), 1)


def reference(amplitudes, gate_matrices, phase_qubits, phase_angles, cut_qubits, cut_angle, path_index):
    total_bits = QUBITS
    index_all = lax.iota(jnp.int32, 2 ** total_bits)
    result = amplitudes
    for layer_number in range(LAYERS):
        if layer_number < GLOBAL_Q:
            result = swap_bits(result, 7 + layer_number, LOCAL_Q + layer_number, total_bits)
            target = 7 + layer_number
        else:
            if layer_number == GLOBAL_Q:
                block_size = 2 ** GLOBAL_Q
                shaped = result.reshape(2, block_size, block_size, 2 ** (LOCAL_Q - GLOBAL_Q))
                result = jnp.swapaxes(shaped, 1, 2).reshape(2, -1)
            target = LOCAL_Q - 2 * GLOBAL_Q + layer_number
        result = apply_gate(result, gate_matrices[layer_number], target, total_bits)
        theta = jnp.zeros((2 ** total_bits,), jnp.float32)
        for pair_number in range(PAIRS):
            first_bit = bit_of(index_all, phase_qubits[layer_number, pair_number, 0])
            second_bit = bit_of(index_all, phase_qubits[layer_number, pair_number, 1])
            theta = theta + phase_angles[layer_number, pair_number] * (first_bit * second_bit).astype(jnp.float32)
        result = rotate(result, theta)
        if layer_number == 0:
            for cut_number in range(CUTS):
                parity = jnp.bitwise_xor(bit_of(index_all, cut_qubits[cut_number, 0]), bit_of(index_all, cut_qubits[cut_number, 1]))
                signs = (1 - 2 * parity).astype(jnp.float32)
                chosen = path_index[cut_number] == 0
                angle_now = cut_angle[cut_number]
                keep_part = jnp.where(chosen, jnp.cos(angle_now), jnp.zeros_like(angle_now))
                turn_part = jnp.where(chosen, jnp.zeros_like(angle_now), jnp.sin(angle_now))
                result = jnp.stack((keep_part * result[0] + turn_part * signs * result[1],
                                    keep_part * result[1] - turn_part * signs * result[0]))
    return result
```

```python
import functools
import math

import jax
import jax.numpy as jnp
from jax import lax
from jax.experimental import pallas as pl
from jax.experimental.pallas import tpu as pltpu
from jax.sharding import PartitionSpec as P

LANES = 128
SUB = 8
MESH = pl.DeviceIdType.MESH


def quarter_sincos(turns):
    whole = jnp.floor(turns + 0.5)
    rest = turns - whole
    square = rest * rest
    half_pi = math.pi / 2
    sin_terms = [(-1) ** k * half_pi ** (2 * k + 1) / math.factorial(2 * k + 1) for k in range(5)]
    cos_terms = [(-1) ** k * half_pi ** (2 * k) / math.factorial(2 * k) for k in range(6)]
    sine = jnp.full_like(square, sin_terms[-1])
    for term in sin_terms[-2::-1]:
        sine = sine * square + term
    sine = sine * rest
    cosine = jnp.full_like(square, cos_terms[-1])
    for term in cos_terms[-2::-1]:
        cosine = cosine * square + term
    count = whole.astype(jnp.int32)
    odd = (count & 1) == 1
    sin_out = jnp.where(odd, cosine, sine)
    cos_out = jnp.where(odd, sine, cosine)
    sin_out = jnp.where((count & 2) == 2, -sin_out, sin_out)
    cos_out = jnp.where(((count + 1) & 2) == 2, -cos_out, cos_out)
    return sin_out, cos_out


def swap_half(value):
    return pltpu.roll(value, LANES // 2, axis=1)


def spread(value, moves):
    total = None
    for a, b in moves:
        term = ((value >> a) & 1) << b
        total = term if total is None else total + term
    return total


def times(a, b):
    return a[0] * b[0] - a[1] * b[1], a[0] * b[1] + a[1] * b[0]


def circuit_kernel(
    g, local_bits, layers, pairs, cuts,
    amp_ref, gate_ref, qubit_in, angle_in, cut_qubit_in, cut_angle_in, path_in, out_ref,
    qubit_ref, angle_ref, cut_qubit_ref, cut_angle_ref, path_ref,
    recv, weights, gates, cos_all, sin_all, x_tab, y_tab, r_tab, mixed, turned,
    send_sem, recv_sem, gate_sem, small_sem, came_sem, go_sem,
):
    n = 2**g
    half, quarter = n // 2, n // 4
    block_bits = local_bits - g - 7
    chunks = 2 ** (block_bits - 3)
    piece = 2 * SUB
    rows = n * SUB
    half_rows = half * SUB
    me = lax.axis_index("hi")
    top = me // half
    spot = lax.rem(me, half)

    def block_rows(owner, chunk):
        return pl.ds(pl.multiple_of((owner * chunks + chunk) * piece, piece), piece)

    def slot_rows(source):
        return pl.ds(pl.multiple_of(source * piece, piece), piece)

    def half_slots(side):
        return pl.ds(pl.multiple_of(side * half * piece, half * piece), half * piece)

    def send(chunk, peer):
        pltpu.make_async_remote_copy(
            src_ref=amp_ref.at[block_rows(peer, chunk)],
            dst_ref=recv.at[chunk, slot_rows(me)],
            send_sem=send_sem.at[chunk],
            recv_sem=recv_sem.at[chunk, top],
            device_id={"hi": peer},
            device_id_type=MESH,
        ).start()

    def arrived(chunk, side):
        here = recv.at[chunk, half_slots(side)]
        pltpu.make_async_copy(here, here, recv_sem.at[chunk, side]).wait()

    def signal(semaphore, peer):
        pl.semaphore_signal(semaphore, inc=1, device_id={"hi": peer}, device_id_type=MESH)

    barrier = pltpu.get_barrier_semaphore()

    @pl.when(top == 0)
    def _():
        for off in range(half):
            signal(barrier, half + lax.rem(spot + off, half))
        for off in range(1, half):
            signal(barrier, lax.rem(spot + off, half))

    smalls = (
        (qubit_in, qubit_ref),
        (angle_in, angle_ref),
        (cut_qubit_in, cut_qubit_ref),
        (cut_angle_in, cut_angle_ref),
        (path_in, path_ref),
    )
    small_copies = [
        pltpu.make_async_copy(source, target, small_sem.at[k])
        for k, (source, target) in enumerate(smalls)
    ]
    for small_copy in small_copies:
        small_copy.start()
    gate_copy = pltpu.make_async_copy(gate_ref, gates, gate_sem)
    gate_copy.start()

    @pl.loop(0, chunks)
    def _(chunk):
        pltpu.make_async_copy(
            amp_ref.at[block_rows(me, chunk)],
            recv.at[chunk, slot_rows(me)],
            recv_sem.at[chunk, top],
        ).start()

    @pl.when(top == 1)
    def _():
        pl.semaphore_wait(barrier, half)
        for off in range(half):
            signal(came_sem.at[spot // quarter], half - 1 - off)

        @pl.loop(0, chunks)
        def _(chunk):
            for level in range(2):
                for off in range(quarter):
                    send(chunk, level * quarter + lax.rem(spot + off, quarter))

    low_lanes = lax.broadcasted_iota(jnp.int32, (64, LANES), 1) < 64

    def make_weights(layer):
        real_t = gates[layer, 0].astype(jnp.float32).T
        imag_t = gates[layer, 1].astype(jnp.float32).T
        for t in range(2):
            real_rows = real_t[t * 64 : (t + 1) * 64]
            imag_rows = imag_t[t * 64 : (t + 1) * 64]
            real_turned, imag_turned = swap_half(real_rows), swap_half(imag_rows)
            parts = (
                (
                    jnp.where(low_lanes, real_rows, imag_turned),
                    jnp.where(low_lanes, real_turned, imag_rows),
                ),
                (
                    jnp.where(low_lanes, -imag_rows, real_turned),
                    jnp.where(low_lanes, -imag_turned, real_rows),
                ),
            )
            for c in range(2):
                for t_out in range(2):
                    weights[
                        layer,
                        t * 128 + c * 64 : t * 128 + c * 64 + 64,
                        t_out * 128 : t_out * 128 + 128,
                    ] = parts[c][t_out].astype(jnp.bfloat16)

    def chunk_row(k):
        return block_bits + 3 + k if 10 + k < 7 + g else 3 + k

    lane = lax.broadcasted_iota(jnp.int32, (SUB, LANES), 1)
    sub = lax.broadcasted_iota(jnp.int32, (SUB, LANES), 0)
    tile_low = lane < 64
    to_quarter = 2.0 / math.pi
    chunk_places = [10 + k for k in range(block_bits - 3)]

    def entered(layer, q):
        if layer < g:
            up = (q >= 7) & (q <= 7 + layer)
            down = (q >= local_bits) & (q <= local_bits + layer)
            moved = local_bits - 7
            return q + jnp.where(up, moved, 0) - jnp.where(down, moved, 0)
        shift = jnp.where(q >= 7, local_bits - 7, 0)
        shift = jnp.where(q >= 7 + g, 0, shift)
        shift = jnp.where(q >= local_bits - g, 7 + g - local_bits, shift)
        shift = jnp.where(q >= local_bits, -g, shift)
        return q + shift

    def make_table(layer):
        if layer < g:
            tile_places = [7, 8, 9]
            row_places = [local_bits + k for k in range(g)]
        else:
            tile_places = [local_bits + k for k in range(3)]
            row_places = [local_bits + k for k in range(3, g)] + [7, 8, 9]
        places = row_places + chunk_places
        masks, angles = [], []
        for k in range(pairs):
            masks.append(
                (jnp.int32(1) << entered(layer, qubit_ref[layer, 0, k]))
                | (jnp.int32(1) << entered(layer, qubit_ref[layer, 1, k]))
            )
            angles.append(angle_ref[layer, k] * to_quarter)

        def total(index, pick):
            turns = jnp.zeros((SUB, LANES), jnp.float32)
            for k in range(pairs):
                mask, angle = pick(masks[k], angles[k])
                turns = turns + jnp.where((index & mask) == mask, angle, 0.0)
            return turns

        tile_index = (
            lane
            + spread(sub, list(enumerate(tile_places)))
            + spread(me, [(k, local_bits - g + k) for k in range(g)])
        )
        turns = [total(tile_index, lambda mask, angle: (mask, angle))]
        for place in places:
            bit = 1 << place
            turns.append(
                total(
                    tile_index | bit,
                    lambda mask, angle: (
                        mask, jnp.where(((mask & bit) != 0) & (mask != bit), angle, 0.0)
                    ),
                )
            )
        row_tiles = 2 ** len(places) // SUB
        for tile in range(row_tiles):
            row_index = spread(sub, list(enumerate(places[:3]))) + sum(
                (1 << place) if (tile >> k) & 1 else 0 for k, place in enumerate(places[3:])
            )
            turns.append(total(row_index, lambda mask, angle: (mask, angle)))
        if layer == 0:
            cut_mask = jnp.int32(0)
            cut_turns = jnp.float32(0)
            cut_size = jnp.full((SUB, LANES), 1.0, jnp.float32)
            for k in range(cuts):
                kept = path_ref[k] == 0
                bits = (jnp.int32(1) << entered(0, cut_qubit_ref[0, k])) ^ (
                    jnp.int32(1) << entered(0, cut_qubit_ref[1, k])
                )
                cut_mask = cut_mask ^ jnp.where(kept, 0, bits)
                cut_turns = cut_turns - jnp.where(kept, 0.0, 1.0)
                sine, cosine = quarter_sincos(
                    jnp.full((SUB, LANES), cut_angle_ref[k], jnp.float32) * to_quarter
                )
                kept_all = jnp.full((SUB, LANES), path_ref[k], jnp.int32) == 0
                cut_size = cut_size * jnp.where(kept_all, cosine, sine)
            folded = tile_index & cut_mask
            for shift in (16, 8, 4, 2, 1):
                folded = folded ^ (folded >> shift)
            turns[0] = turns[0] + cut_turns + ((folded & 1) * 2).astype(jnp.float32)
            for k, place in enumerate(places):
                turns[1 + k] = turns[1 + k] + jnp.where((cut_mask & (1 << place)) != 0, 2.0, 0.0)
        sine, cosine = quarter_sincos(jnp.stack(turns))
        waves = [(cosine[k], sine[k]) for k in range(len(turns))]
        base, steps, row_waves = waves[0], waves[1 : 1 + len(places)], waves[1 + len(places) :]
        if layer == 0:
            base = (base[0] * cut_size, base[1] * cut_size)
        for tile in range(row_tiles):
            for part in range(2):
                r_tab[layer, part, tile * SUB : (tile + 1) * SUB] = row_waves[tile][part]
        x_waves = [base]
        for step in steps[:3]:
            x_waves = x_waves + [times(wave, step) for wave in x_waves]
        y_waves = [None]
        for step in steps[3:]:
            y_waves = y_waves + [
                step if wave is None else times(wave, step) for wave in y_waves
            ]
        y_waves[0] = (jnp.ones((SUB, LANES), jnp.float32), jnp.zeros((SUB, LANES), jnp.float32))
        for tab, values in ((x_tab, x_waves), (y_tab, y_waves)):
            for k, wave in enumerate(values):
                for part in range(2):
                    tab[layer, k, part] = wave[part]
        per_chunk = n // SUB

        @pl.loop(0, row_tiles)
        def _(y):
            chunk = y // per_chunk
            start = lax.rem(y, per_chunk) * (SUB * SUB)
            y_wave = (y_tab[layer, y, 0], y_tab[layer, y, 1])
            for x in range(SUB):
                row = pl.ds(y * SUB + x, 1)
                row_wave = tuple(
                    jnp.broadcast_to(r_tab[layer, part, row, :], (SUB, LANES)) for part in range(2)
                )
                x_wave = (x_tab[layer, x, 0], x_tab[layer, x, 1])
                cosine, sine = times(times(x_wave, y_wave), row_wave)
                sine_turned, cosine_turned = swap_half(sine), swap_half(cosine)
                at = pl.ds(pl.multiple_of(start + x * SUB, SUB), SUB)
                cos_all[layer, chunk, 0, at] = jnp.where(tile_low, cosine, cosine_turned)
                cos_all[layer, chunk, 1, at] = jnp.where(tile_low, cosine_turned, cosine)
                sin_all[layer, chunk, 0, at] = jnp.where(tile_low, -sine, sine_turned)
                sin_all[layer, chunk, 1, at] = jnp.where(tile_low, -sine_turned, sine)

    for small_copy in small_copies:
        small_copy.wait()
    for layer in range(3):
        make_table(layer)

    @pl.when(top == 0)
    def _():
        pl.semaphore_wait(barrier, half - 1)

        @pl.loop(0, chunks)
        def _(chunk):
            for off in range(1, half):
                send(chunk, lax.rem(spot + off, half))

        pl.semaphore_wait(came_sem.at[0], quarter)
        pl.semaphore_wait(came_sem.at[1], quarter)
        signal(go_sem, me + half)

        @pl.loop(0, chunks)
        def _(chunk):
            for level in range(2):
                for off in range(quarter):
                    send(chunk, half + level * quarter + lax.rem(spot + off, quarter))

    gate_copy.wait()

    @pl.loop(0, layers)
    def _(layer):
        make_weights(layer)

    for layer in range(3, layers):
        make_table(layer)

    @pl.when(top == 1)
    def _():
        pl.semaphore_wait(go_sem, 1)

        @pl.loop(0, chunks)
        def _(chunk):
            for off in range(1, half):
                send(chunk, half + lax.rem(spot + off, half))

    def layer_step(state, layer, outer, inner, cosine, sine):
        count = outer * inner * 2
        shaped = state.reshape(2, outer, 2, inner, LANES)
        joined = jnp.concatenate(
            (shaped[:, :, 0].reshape(count, LANES), shaped[:, :, 1].reshape(count, LANES)), axis=1
        )
        high = joined.astype(jnp.bfloat16)
        rest = (joined - high.astype(jnp.float32)).astype(jnp.bfloat16)
        gate = weights[layer]
        both = jnp.dot(
            jnp.concatenate((high, rest), axis=0), gate, preferred_element_type=jnp.float32
        )
        product = both[:count] + both[count:]
        back = jnp.stack(
            (
                product[:, :LANES].reshape(2, outer, inner, LANES),
                product[:, LANES:].reshape(2, outer, inner, LANES),
            ),
            axis=2,
        ).reshape(2 * count, LANES)
        return back * cosine + swap_half(back) * sine

    half_low = lax.broadcasted_iota(jnp.int32, (half_rows, LANES), 1) < 64
    flat_low = lax.broadcasted_iota(jnp.int32, (rows, LANES), 1) < 64

    def first_layers(chunk, side):
        start = pl.multiple_of(side * half * piece, half * piece)
        real = recv[chunk, pl.ds(start, half_rows, stride=2), :]
        imag = recv[chunk, pl.ds(start + 1, half_rows, stride=2), :]
        state = jnp.concatenate(
            (
                jnp.where(half_low, real, swap_half(imag)),
                jnp.where(half_low, swap_half(real), imag),
            ),
            axis=0,
        )
        mine = pl.ds(pl.multiple_of(side * half_rows, half_rows), half_rows)
        for layer in range(g - 1):
            cosine = cos_all[layer, chunk, :, mine].reshape(2 * half_rows, LANES)
            sine = sin_all[layer, chunk, :, mine].reshape(2 * half_rows, LANES)
            state = layer_step(
                state, layer, 2 ** (g - 2 - layer), 2**layer * SUB, cosine, sine
            )
        mixed[chunk, 0, mine] = state[:half_rows]
        mixed[chunk, 1, mine] = state[half_rows:]

    @pl.loop(0, chunks)
    def _(chunk):
        arrived(chunk, top)
        first_layers(chunk, top)

    @pl.loop(0, chunks)
    def _(chunk):
        arrived(chunk, 1 - top)
        first_layers(chunk, 1 - top)
        state = mixed[chunk].reshape(2 * rows, LANES)

        def whole_step(state, layer, outer, inner):
            cosine = cos_all[layer, chunk].reshape(2 * rows, LANES)
            sine = sin_all[layer, chunk].reshape(2 * rows, LANES)
            return layer_step(state, layer, outer, inner, cosine, sine)

        turned[...] = whole_step(state, g - 1, 1, half * SUB)
        state = jnp.concatenate(
            [
                turned[pl.ds(b * rows + low, n, stride=SUB), :]
                for b in range(2)
                for low in range(SUB)
            ],
            axis=0,
        )
        for layer in range(g, layers):
            k = layer - g
            state = whole_step(state, layer, 2 ** (2 - k), 2**k * n)
        zero, one = state[:rows], state[rows:]
        real = jnp.where(flat_low, zero, swap_half(one))
        imag = jnp.where(flat_low, swap_half(zero), one)
        base = spread(chunk, [(k, chunk_row(k)) for k in range(block_bits - 3)])
        for low in range(SUB):
            start = pl.multiple_of(2 * (base + (low << block_bits)), 2 * n)
            out_ref[pl.ds(start, n, stride=2), :] = real[low * n : (low + 1) * n]
            out_ref[pl.ds(start + 1, n, stride=2), :] = imag[low * n : (low + 1) * n]

    @pl.loop(0, chunks)
    def _(chunk):
        gone = amp_ref.at[pl.ds(0, (n - 1) * piece)]
        pltpu.make_async_remote_copy(
            src_ref=gone,
            dst_ref=recv.at[chunk, pl.ds(0, (n - 1) * piece)],
            send_sem=send_sem.at[chunk],
            recv_sem=recv_sem.at[chunk, 0],
            device_id={"hi": lax.rem(me + 1, n)},
            device_id_type=MESH,
        ).wait_send()


def one_exchange(
    amplitudes, gate_matrices, phase_qubits, phase_angles, cut_qubits, cut_angle, path_index
):
    g = lax.axis_size("hi").bit_length() - 1
    amp_count = amplitudes.shape[1]
    local_bits = amp_count.bit_length() - 1
    layers, pairs = phase_angles.shape
    cuts = cut_angle.shape[0]
    n = 2**g
    chunks = 2 ** (local_bits - g - 10)
    rows = n * SUB
    all_rows = amp_count // LANES
    row_tiles = n * chunks // SUB
    whole = amplitudes.reshape(2, all_rows, LANES).transpose(1, 0, 2).reshape(2 * all_rows, LANES)
    hbm = pl.BlockSpec(memory_space=pltpu.HBM)
    result = pl.pallas_call(
        functools.partial(circuit_kernel, g, local_bits, layers, pairs, cuts),
        out_shape=pltpu.VMEM((2 * all_rows, LANES), jnp.float32),
        in_specs=[hbm] * 7,
        out_specs=pl.BlockSpec(memory_space=pltpu.VMEM),
        scratch_shapes=[
            pltpu.SMEM((layers, 2, pairs), jnp.int32),
            pltpu.SMEM(phase_angles.shape, jnp.float32),
            pltpu.SMEM((2, cuts), jnp.int32),
            pltpu.SMEM(cut_angle.shape, jnp.float32),
            pltpu.SMEM(path_index.shape, jnp.int32),
            pltpu.VMEM((chunks, 2 * rows, LANES), jnp.float32),
            pltpu.VMEM((layers, 256, 256), jnp.bfloat16),
            pltpu.VMEM(gate_matrices.shape, jnp.bfloat16),
            pltpu.VMEM((layers, chunks, 2, rows, LANES), jnp.float32),
            pltpu.VMEM((layers, chunks, 2, rows, LANES), jnp.float32),
            pltpu.VMEM((layers, SUB, 2, SUB, LANES), jnp.float32),
            pltpu.VMEM((layers, row_tiles, 2, SUB, LANES), jnp.float32),
            pltpu.VMEM((layers, 2, row_tiles * SUB, LANES), jnp.float32),
            pltpu.VMEM((chunks, 2, rows, LANES), jnp.float32),
            pltpu.VMEM((2 * rows, LANES), jnp.float32),
            pltpu.SemaphoreType.DMA((chunks,)),
            pltpu.SemaphoreType.DMA((chunks, 2)),
            pltpu.SemaphoreType.DMA,
            pltpu.SemaphoreType.DMA((5,)),
            pltpu.SemaphoreType.REGULAR((2,)),
            pltpu.SemaphoreType.REGULAR,
        ],
        compiler_params=pltpu.CompilerParams(collective_id=0, has_side_effects=True),
    )(
        whole, gate_matrices, phase_qubits.transpose(0, 2, 1), phase_angles,
        cut_qubits.transpose(1, 0), cut_angle, path_index,
    )
    return result.reshape(all_rows, 2, LANES).transpose(1, 0, 2).reshape(2, amp_count)


def from_partner(value, axis, bit):
    return lax.ppermute(value, axis, [(i, i ^ 1 << bit) for i in range(lax.axis_size(axis))])


def real_form(matrix):
    real_part = matrix[0].astype(jnp.float32)
    imag_part = matrix[1].astype(jnp.float32)
    upper_rows = jnp.stack((real_part, -imag_part), axis=1)
    lower_rows = jnp.stack((imag_part, real_part), axis=1)
    stacked = jnp.stack((upper_rows, lower_rows), axis=0)
    return stacked.reshape(2, 2, 64, 2, 2, 64)


def apply_gate(amps_now, matrix, target, local_bits):
    shaped = amps_now.reshape(2, 2 ** (local_bits - 1 - target), 2, 2 ** (target - 7), 2, 64)
    result = jnp.einsum(
        "wxyzbd,zabced->waxcey", real_form(matrix), shaped, precision=lax.Precision.HIGHEST
    )
    return result.reshape(2, -1)


def rotate(amps_now, theta):
    cosine = jnp.cos(theta)
    sine = jnp.sin(theta)
    return jnp.stack(
        (cosine * amps_now[0] - sine * amps_now[1], sine * amps_now[0] + cosine * amps_now[1])
    )


def bit_of(index_all, qubit):
    return jnp.bitwise_and(jnp.right_shift(index_all, qubit), 1)


def located(qubit, first_open, global_count, local_bits):
    moved_up = (qubit >= 7 + first_open) & (qubit < 7 + global_count)
    moved_down = (qubit >= local_bits + first_open) & (qubit < local_bits + global_count)
    return jnp.where(
        moved_up, qubit - 7 + local_bits, jnp.where(moved_down, qubit - local_bits + 7, qubit)
    )


def enter_qubit(amps_now, bit_number, local_bits, device_place):
    shaped = amps_now.reshape(2, 2 ** (local_bits - 8 - bit_number), 2, 2**bit_number, 128)
    zero_half = shaped[:, :, 0]
    one_half = shaped[:, :, 1]
    upper_side = jnp.bitwise_and(jnp.right_shift(device_place, bit_number), 1) == 1
    kept_half = jnp.where(upper_side, one_half, zero_half)
    sent_half = jnp.where(upper_side, zero_half, one_half)
    came_half = from_partner(sent_half, "hi", bit_number)
    new_zero = jnp.where(upper_side, came_half, kept_half)
    new_one = jnp.where(upper_side, kept_half, came_half)
    return jnp.stack((new_zero, new_one), axis=2).reshape(2, -1)


def shards(
    amplitudes, gate_matrices, phase_qubits, phase_angles, cut_qubits, cut_angle, path_index
):
    global_count = lax.axis_size("hi").bit_length() - 1
    amp_count = amplitudes.shape[1]
    local_bits = amp_count.bit_length() - 1
    device_place = lax.axis_index("hi")
    index_all = device_place * amp_count + lax.iota(jnp.int32, amp_count)
    layer_count = gate_matrices.shape[0]
    result = amplitudes
    for layer_number in range(layer_count):
        if layer_number < global_count:
            result = enter_qubit(result, layer_number, local_bits, device_place)
            target = 7 + layer_number
        else:
            if layer_number == global_count:
                shaped = result.reshape(2, 2**global_count, 2 ** (local_bits - global_count))
                result = lax.all_to_all(
                    shaped, "hi", split_axis=1, concat_axis=1, tiled=True
                ).reshape(2, -1)
            target = local_bits - 2 * global_count + layer_number
        result = apply_gate(result, gate_matrices[layer_number], target, local_bits)
        theta = jnp.zeros((amp_count,), jnp.float32)
        for pair_number in range(phase_qubits.shape[1]):
            first_pos = located(
                phase_qubits[layer_number, pair_number, 0], global_count, global_count, local_bits
            )
            second_pos = located(
                phase_qubits[layer_number, pair_number, 1], global_count, global_count, local_bits
            )
            both_bits = bit_of(index_all, first_pos) * bit_of(index_all, second_pos)
            theta = theta + phase_angles[layer_number, pair_number] * both_bits.astype(jnp.float32)
        result = rotate(result, theta)
        if layer_number == 0:
            for cut_number in range(cut_qubits.shape[0]):
                first_cut = located(
                    cut_qubits[cut_number, 0], global_count, global_count, local_bits
                )
                second_cut = located(
                    cut_qubits[cut_number, 1], global_count, global_count, local_bits
                )
                parity = jnp.bitwise_xor(
                    bit_of(index_all, first_cut), bit_of(index_all, second_cut)
                )
                signs = (1 - 2 * parity).astype(jnp.float32)
                chosen = path_index[cut_number] == 0
                angle_now = cut_angle[cut_number]
                keep_part = jnp.where(chosen, jnp.cos(angle_now), jnp.zeros_like(angle_now))
                turn_part = jnp.where(chosen, jnp.zeros_like(angle_now), jnp.sin(angle_now))
                result = jnp.stack(
                    (
                        keep_part * result[0] + turn_part * signs * result[1],
                        keep_part * result[1] - turn_part * signs * result[0],
                    )
                )
    return result


def any_slice(amplitudes, gate_matrices, *rest):
    g = lax.axis_size("hi").bit_length() - 1
    local_bits = amplitudes.shape[1].bit_length() - 1
    late_layers = gate_matrices.shape[0] - g
    fits = 3 <= g <= local_bits - g - 7 and local_bits - g >= 11 and 0 < late_layers <= 3
    plan = one_exchange if fits else shards
    return plan(amplitudes, gate_matrices, *rest)


def solution(mesh):
    placed = (
        P(None, ("paths", "hi")),
        P(),
        P("paths", None, None),
        P("paths", None),
        P("paths", None),
        P("paths"),
        P("paths"),
    )
    return jax.shard_map(
        any_slice, mesh=mesh, in_specs=placed, out_specs=P(None, ("paths", "hi")), check_vma=False
    )
```

```python
import functools
import math

import jax
import jax.numpy as jnp
from jax import lax
from jax.experimental import pallas as pl
from jax.experimental.pallas import tpu as pltpu
from jax.sharding import PartitionSpec as P

LANES = 128
SUB = 8
MESH = pl.DeviceIdType.MESH


def quarter_sincos(turns):
    whole = jnp.floor(turns + 0.5)
    rest = turns - whole
    square = rest * rest
    half_pi = math.pi / 2
    sin_terms = [(-1) ** k * half_pi ** (2 * k + 1) / math.factorial(2 * k + 1) for k in range(5)]
    cos_terms = [(-1) ** k * half_pi ** (2 * k) / math.factorial(2 * k) for k in range(6)]
    sine = jnp.full_like(square, sin_terms[-1])
    for term in sin_terms[-2::-1]:
        sine = sine * square + term
    sine = sine * rest
    cosine = jnp.full_like(square, cos_terms[-1])
    for term in cos_terms[-2::-1]:
        cosine = cosine * square + term
    count = whole.astype(jnp.int32)
    odd = (count & 1) == 1
    sin_out = jnp.where(odd, cosine, sine)
    cos_out = jnp.where(odd, sine, cosine)
    sin_out = jnp.where((count & 2) == 2, -sin_out, sin_out)
    cos_out = jnp.where(((count + 1) & 2) == 2, -cos_out, cos_out)
    return sin_out, cos_out


def swap_half(value):
    return pltpu.roll(value, LANES // 2, axis=1)


def spread(value, moves):
    total = None
    for a, b in moves:
        term = ((value >> a) & 1) << b
        total = term if total is None else total + term
    return total


def times(a, b):
    return a[0] * b[0] - a[1] * b[1], a[0] * b[1] + a[1] * b[0]


def circuit_kernel(
    g, local_bits, layers, pairs, cuts,
    amp_ref, gate_ref, qubit_in, angle_in, cut_qubit_in, cut_angle_in, path_in, out_ref,
    qubit_ref, angle_ref, cut_qubit_ref, cut_angle_ref, path_ref,
    recv, weights, gates, cos_all, sin_all, x_tab, y_tab, r_tab, mixed, turned,
    send_sem, recv_sem, gate_sem, small_sem, came_sem, go_sem,
):
    n = 2**g
    half, quarter = n // 2, n // 4
    block_bits = local_bits - g - 7
    chunks = 2 ** (block_bits - 3)
    piece = 2 * SUB
    rows = n * SUB
    half_rows = half * SUB
    me = lax.axis_index("hi")
    top = me // half
    spot = lax.rem(me, half)

    def block_rows(owner, chunk):
        return pl.ds(pl.multiple_of((owner * chunks + chunk) * piece, piece), piece)

    def slot_rows(source):
        return pl.ds(pl.multiple_of(source * piece, piece), piece)

    def half_slots(side):
        return pl.ds(pl.multiple_of(side * half * piece, half * piece), half * piece)

    def send(chunk, peer):
        pltpu.make_async_remote_copy(
            src_ref=amp_ref.at[block_rows(peer, chunk)],
            dst_ref=recv.at[chunk, slot_rows(me)],
            send_sem=send_sem.at[chunk],
            recv_sem=recv_sem.at[chunk, top],
            device_id={"hi": peer},
            device_id_type=MESH,
        ).start()

    def arrived(chunk, side):
        here = recv.at[chunk, half_slots(side)]
        pltpu.make_async_copy(here, here, recv_sem.at[chunk, side]).wait()

    def signal(semaphore, peer):
        pl.semaphore_signal(semaphore, inc=1, device_id={"hi": peer}, device_id_type=MESH)

    barrier = pltpu.get_barrier_semaphore()

    @pl.when(top == 0)
    def _():
        for off in range(half):
            signal(barrier, half + lax.rem(spot + off, half))
        for off in range(1, half):
            signal(barrier, lax.rem(spot + off, half))

    smalls = (
        (qubit_in, qubit_ref),
        (angle_in, angle_ref),
        (cut_qubit_in, cut_qubit_ref),
        (cut_angle_in, cut_angle_ref),
        (path_in, path_ref),
    )
    small_copies = [
        pltpu.make_async_copy(source, target, small_sem.at[k])
        for k, (source, target) in enumerate(smalls)
    ]
    for small_copy in small_copies:
        small_copy.start()
    gate_copy = pltpu.make_async_copy(gate_ref, gates, gate_sem)
    gate_copy.start()

    @pl.loop(0, chunks)
    def _(chunk):
        pltpu.make_async_copy(
            amp_ref.at[block_rows(me, chunk)],
            recv.at[chunk, slot_rows(me)],
            recv_sem.at[chunk, top],
        ).start()

    def send_near(first, last):
        @pl.loop(first, last)
        def _(chunk):
            for off in range(1, half):
                send(chunk, top * half + lax.rem(spot + off, half))

    def send_across(first, last, levels):
        @pl.loop(first, last)
        def _(chunk):
            for level in levels:
                for off in range(quarter):
                    send(chunk, (1 - top) * half + level * quarter + lax.rem(spot + off, quarter))

    def across_chips():
        for level in range(2):
            for off in range(quarter // 2):
                yield level * (quarter // 2) + lax.rem(spot // 2 + off, quarter // 2)

    def send_chip(chunk, chip):
        for off in range(2):
            send(chunk, (1 - top) * half + chip * 2 + lax.rem(spot + off, 2))

    @pl.when(top == 1)
    def _():
        pl.semaphore_wait(barrier, half)
        for off in range(half):
            signal(came_sem.at[spot // 2], half - 1 - off)
        send_across(0, chunks, (0,))
        send_across(0, chunks, (1,))

    low_lanes = lax.broadcasted_iota(jnp.int32, (64, LANES), 1) < 64
    blank = jnp.zeros((64, LANES), jnp.float32)

    def make_weights(layer):
        flat = [gates[layer, part].astype(jnp.float32).T for part in range(2)]
        for t in range(2):
            plain = [part[t * 64 : (t + 1) * 64] for part in flat]
            turned_part = [swap_half(part) for part in plain]
            for c in range(2):
                for t_out in range(2):
                    for c_out in range(2):
                        low_from, high_from = (
                            (plain, turned_part) if t_out == 0 else (turned_part, plain)
                        )
                        part = c ^ c_out
                        upper = jnp.where(low_lanes, low_from[part], blank)
                        lower = jnp.where(low_lanes, blank, high_from[part])
                        if c == 1 and c_out == 0:
                            upper, lower = -upper, -lower
                        block = jnp.concatenate((upper, lower), axis=0).astype(jnp.bfloat16)
                        row, column = (2 * t + c) * LANES, (2 * t_out + c_out) * LANES
                        weights[layer, row : row + LANES, column : column + LANES] = block

    def chunk_row(k):
        return block_bits + 3 + k if 10 + k < 7 + g else 3 + k

    lane = lax.broadcasted_iota(jnp.int32, (SUB, LANES), 1)
    sub = lax.broadcasted_iota(jnp.int32, (SUB, LANES), 0)
    to_quarter = 2.0 / math.pi
    chunk_places = [10 + k for k in range(block_bits - 3)]

    def entered(layer, q):
        if layer < g:
            up = (q >= 7) & (q <= 7 + layer)
            down = (q >= local_bits) & (q <= local_bits + layer)
            moved = local_bits - 7
            return q + jnp.where(up, moved, 0) - jnp.where(down, moved, 0)
        shift = jnp.where(q >= 7, local_bits - 7, 0)
        shift = jnp.where(q >= 7 + g, 0, shift)
        shift = jnp.where(q >= local_bits - g, 7 + g - local_bits, shift)
        shift = jnp.where(q >= local_bits, -g, shift)
        return q + shift

    def make_table(layer):
        if layer < g:
            tile_places = [7, 8, 9]
            row_places = [local_bits + k for k in range(g)]
        else:
            tile_places = [local_bits + k for k in range(3)]
            row_places = [local_bits + k for k in range(3, g)] + [7, 8, 9]
        places = row_places + chunk_places
        masks, angles = [], []
        for k in range(pairs):
            masks.append(
                (jnp.int32(1) << entered(layer, qubit_ref[layer, 0, k]))
                | (jnp.int32(1) << entered(layer, qubit_ref[layer, 1, k]))
            )
            angles.append(angle_ref[layer, k] * to_quarter)

        def total(index, pick):
            turns = jnp.zeros((SUB, LANES), jnp.float32)
            for k in range(pairs):
                mask, angle = pick(masks[k], angles[k])
                turns = turns + jnp.where((index & mask) == mask, angle, 0.0)
            return turns

        tile_index = (
            lane
            + spread(sub, list(enumerate(tile_places)))
            + spread(me, [(k, local_bits - g + k) for k in range(g)])
        )
        turns = [total(tile_index, lambda mask, angle: (mask, angle))]
        for place in places:
            bit = 1 << place
            turns.append(
                total(
                    tile_index | bit,
                    lambda mask, angle: (
                        mask, jnp.where(((mask & bit) != 0) & (mask != bit), angle, 0.0)
                    ),
                )
            )
        row_tiles = 2 ** len(places) // SUB
        for tile in range(row_tiles):
            row_index = spread(sub, list(enumerate(places[:3]))) + sum(
                (1 << place) if (tile >> k) & 1 else 0 for k, place in enumerate(places[3:])
            )
            turns.append(total(row_index, lambda mask, angle: (mask, angle)))
        if layer == 0:
            cut_mask = jnp.int32(0)
            cut_turns = jnp.float32(0)
            cut_size = jnp.full((SUB, LANES), 1.0, jnp.float32)
            for k in range(cuts):
                kept = path_ref[k] == 0
                bits = (jnp.int32(1) << entered(0, cut_qubit_ref[0, k])) ^ (
                    jnp.int32(1) << entered(0, cut_qubit_ref[1, k])
                )
                cut_mask = cut_mask ^ jnp.where(kept, 0, bits)
                cut_turns = cut_turns - jnp.where(kept, 0.0, 1.0)
                sine, cosine = quarter_sincos(
                    jnp.full((SUB, LANES), cut_angle_ref[k], jnp.float32) * to_quarter
                )
                kept_all = jnp.full((SUB, LANES), path_ref[k], jnp.int32) == 0
                cut_size = cut_size * jnp.where(kept_all, cosine, sine)
            folded = tile_index & cut_mask
            for shift in (16, 8, 4, 2, 1):
                folded = folded ^ (folded >> shift)
            turns[0] = turns[0] + cut_turns + ((folded & 1) * 2).astype(jnp.float32)
            for k, place in enumerate(places):
                turns[1 + k] = turns[1 + k] + jnp.where((cut_mask & (1 << place)) != 0, 2.0, 0.0)
        sine, cosine = quarter_sincos(jnp.stack(turns))
        waves = [(cosine[k], sine[k]) for k in range(len(turns))]
        base, steps, row_waves = waves[0], waves[1 : 1 + len(places)], waves[1 + len(places) :]
        if layer == 0:
            base = (base[0] * cut_size, base[1] * cut_size)
        for tile in range(row_tiles):
            for part in range(2):
                r_tab[layer, part, tile * SUB : (tile + 1) * SUB] = row_waves[tile][part]
        x_waves = [base]
        for step in steps[:3]:
            x_waves = x_waves + [times(wave, step) for wave in x_waves]
        y_waves = [None]
        for step in steps[3:]:
            y_waves = y_waves + [
                step if wave is None else times(wave, step) for wave in y_waves
            ]
        y_waves[0] = (jnp.ones((SUB, LANES), jnp.float32), jnp.zeros((SUB, LANES), jnp.float32))
        for tab, values in ((x_tab, x_waves), (y_tab, y_waves)):
            for k, wave in enumerate(values):
                for part in range(2):
                    tab[layer, k, part] = wave[part]
        per_chunk = n // SUB

        @pl.loop(0, row_tiles)
        def _(y):
            chunk = y // per_chunk
            start = lax.rem(y, per_chunk) * (SUB * SUB)
            y_wave = (y_tab[layer, y, 0], y_tab[layer, y, 1])
            for x in range(SUB):
                row = pl.ds(y * SUB + x, 1)
                row_wave = tuple(
                    jnp.broadcast_to(r_tab[layer, part, row, :], (SUB, LANES)) for part in range(2)
                )
                x_wave = (x_tab[layer, x, 0], x_tab[layer, x, 1])
                cosine, sine = times(times(x_wave, y_wave), row_wave)
                at = pl.ds(pl.multiple_of(start + x * SUB, SUB), SUB)
                cos_all[layer, chunk, at] = cosine
                sin_all[layer, chunk, at] = sine

    @pl.when(top == 0)
    def _():
        pl.semaphore_wait(barrier, half - 1)

    for small_copy in small_copies:
        small_copy.wait()

    for layer in range(0, 1):
        make_table(layer)

    @pl.when(top == 0)
    def _():
        for chip in across_chips():
            pl.semaphore_wait(came_sem.at[chip], 2)
            send_chip(0, chip)
        signal(go_sem, me + half)
        send_near(0, chunks)

        @pl.loop(1, chunks)
        def _(chunk):
            for chip in across_chips():
                send_chip(chunk, chip)

    for layer in range(1, 3):
        make_table(layer)

    @pl.when(top == 1)
    def _():
        pl.semaphore_wait(go_sem, 1)
        send_near(0, chunks)

    for layer in range(3, 6):
        make_table(layer)

    gate_copy.wait()

    @pl.loop(0, layers)
    def _(layer):
        make_weights(layer)

    def layer_step(state, layer, outer, inner, cosine, sine):
        count = outer * inner

        def pieces(value):
            shaped = value.reshape(outer, 2, inner, LANES)
            return [shaped[:, t].reshape(count, LANES) for t in range(2)]

        def whole(parts):
            shaped = [part.reshape(outer, inner, LANES) for part in parts]
            return jnp.stack(shaped, axis=1).reshape(2 * count, LANES)

        real, imag = pieces(state[0]), pieces(state[1])
        joined = jnp.concatenate((real[0], imag[0], real[1], imag[1]), axis=1)
        high = joined.astype(jnp.bfloat16)
        rest = (joined - high.astype(jnp.float32)).astype(jnp.bfloat16)
        both = jnp.dot(
            jnp.concatenate((high, rest), axis=0),
            weights[layer],
            preferred_element_type=jnp.float32,
        )
        product = both[:count] + both[count:]
        columns = [product[:, k * LANES : (k + 1) * LANES] for k in range(4)]
        return times((whole(columns[0::2]), whole(columns[1::2])), (cosine, sine))

    def first_layers(batch, side):
        start = pl.multiple_of(side * half * piece, half * piece)
        mine = pl.ds(pl.multiple_of(side * half_rows, half_rows), half_rows)

        def joined_rows(read):
            return jnp.concatenate([read(chunk) for chunk in batch], axis=0)

        state = tuple(
            joined_rows(lambda chunk: recv[chunk, pl.ds(start + c, half_rows, stride=2), :])
            for c in range(2)
        )
        for layer in range(g - 1):
            cosine = joined_rows(lambda chunk: cos_all[layer, chunk, mine])
            sine = joined_rows(lambda chunk: sin_all[layer, chunk, mine])
            outer = len(batch) * 2 ** (g - 2 - layer)
            state = layer_step(state, layer, outer, 2**layer * SUB, cosine, sine)
        for k, chunk in enumerate(batch):
            for c in range(2):
                mixed[chunk, c, mine] = state[c][k * half_rows : (k + 1) * half_rows]

    for chunk in range(chunks):
        arrived(chunk, top)
    first_layers(range(chunks), top)

    def last_layers(batch):
        def whole_step(state, layer, outer, inner):
            cosine, sine = (
                jnp.concatenate([table[layer, chunk] for chunk in batch], axis=0)
                for table in (cos_all, sin_all)
            )
            return layer_step(state, layer, len(batch) * outer, inner, cosine, sine)

        state = tuple(
            jnp.concatenate([mixed[chunk, c] for chunk in batch], axis=0) for c in range(2)
        )
        state = whole_step(state, g - 1, 1, half * SUB)
        for c in range(2):
            for k in range(len(batch)):
                turned[k, c] = state[c][k * rows : (k + 1) * rows]
        state = tuple(
            jnp.concatenate(
                [
                    turned[k, c, pl.ds(low, n, stride=SUB), :]
                    for k in range(len(batch))
                    for low in range(SUB)
                ],
                axis=0,
            )
            for c in range(2)
        )
        for layer in range(g, layers):
            k = layer - g
            state = whole_step(state, layer, 2 ** (2 - k), 2**k * n)
        for k, chunk in enumerate(batch):
            base = spread(chunk, [(k, chunk_row(k)) for k in range(block_bits - 3)])
            for low in range(SUB):
                start = pl.multiple_of(2 * (base + (low << block_bits)), 2 * n)
                for c in range(2):
                    out_ref[pl.ds(start + c, n, stride=2), :] = state[c][
                        k * rows + low * n : k * rows + (low + 1) * n
                    ]

    for batch in [[0,1],[2,3]]:
        for chunk in batch:
            arrived(chunk, 1 - top)
        first_layers(batch, 1 - top)
        last_layers(batch)

    @pl.loop(0, chunks)
    def _(chunk):
        gone = amp_ref.at[pl.ds(0, (n - 1) * piece)]
        pltpu.make_async_remote_copy(
            src_ref=gone,
            dst_ref=recv.at[chunk, pl.ds(0, (n - 1) * piece)],
            send_sem=send_sem.at[chunk],
            recv_sem=recv_sem.at[chunk, 0],
            device_id={"hi": lax.rem(me + 1, n)},
            device_id_type=MESH,
        ).wait_send()


def one_exchange(
    amplitudes, gate_matrices, phase_qubits, phase_angles, cut_qubits, cut_angle, path_index
):
    g = lax.axis_size("hi").bit_length() - 1
    amp_count = amplitudes.shape[1]
    local_bits = amp_count.bit_length() - 1
    layers, pairs = phase_angles.shape
    cuts = cut_angle.shape[0]
    n = 2**g
    chunks = 2 ** (local_bits - g - 10)
    rows = n * SUB
    all_rows = amp_count // LANES
    row_tiles = n * chunks // SUB
    whole = amplitudes.reshape(2, all_rows, LANES).transpose(1, 0, 2).reshape(2 * all_rows, LANES)
    hbm = pl.BlockSpec(memory_space=pltpu.HBM)
    result = pl.pallas_call(
        functools.partial(circuit_kernel, g, local_bits, layers, pairs, cuts),
        out_shape=pltpu.VMEM((2 * all_rows, LANES), jnp.float32),
        in_specs=[hbm] * 7,
        out_specs=pl.BlockSpec(memory_space=pltpu.VMEM),
        scratch_shapes=[
            pltpu.SMEM((layers, 2, pairs), jnp.int32),
            pltpu.SMEM(phase_angles.shape, jnp.float32),
            pltpu.SMEM((2, cuts), jnp.int32),
            pltpu.SMEM(cut_angle.shape, jnp.float32),
            pltpu.SMEM(path_index.shape, jnp.int32),
            pltpu.VMEM((chunks, 2 * rows, LANES), jnp.float32),
            pltpu.VMEM((layers, 512, 512), jnp.bfloat16),
            pltpu.VMEM(gate_matrices.shape, jnp.bfloat16),
            pltpu.VMEM((layers, chunks, rows, LANES), jnp.float32),
            pltpu.VMEM((layers, chunks, rows, LANES), jnp.float32),
            pltpu.VMEM((layers, SUB, 2, SUB, LANES), jnp.float32),
            pltpu.VMEM((layers, row_tiles, 2, SUB, LANES), jnp.float32),
            pltpu.VMEM((layers, 2, row_tiles * SUB, LANES), jnp.float32),
            pltpu.VMEM((chunks, 2, rows, LANES), jnp.float32),
            pltpu.VMEM((chunks, 2, rows, LANES), jnp.float32),
            pltpu.SemaphoreType.DMA((chunks,)),
            pltpu.SemaphoreType.DMA((chunks, 2)),
            pltpu.SemaphoreType.DMA,
            pltpu.SemaphoreType.DMA((5,)),
            pltpu.SemaphoreType.REGULAR((n // 4,)),
            pltpu.SemaphoreType.REGULAR,
        ],
        compiler_params=pltpu.CompilerParams(collective_id=0, has_side_effects=True),
    )(
        whole, gate_matrices, phase_qubits.transpose(0, 2, 1), phase_angles,
        cut_qubits.transpose(1, 0), cut_angle, path_index,
    )
    return result.reshape(all_rows, 2, LANES).transpose(1, 0, 2).reshape(2, amp_count)


def from_partner(value, axis, bit):
    return lax.ppermute(value, axis, [(i, i ^ 1 << bit) for i in range(lax.axis_size(axis))])


def real_form(matrix):
    real_part = matrix[0].astype(jnp.float32)
    imag_part = matrix[1].astype(jnp.float32)
    upper_rows = jnp.stack((real_part, -imag_part), axis=1)
    lower_rows = jnp.stack((imag_part, real_part), axis=1)
    stacked = jnp.stack((upper_rows, lower_rows), axis=0)
    return stacked.reshape(2, 2, 64, 2, 2, 64)


def apply_gate(amps_now, matrix, target, local_bits):
    shaped = amps_now.reshape(2, 2 ** (local_bits - 1 - target), 2, 2 ** (target - 7), 2, 64)
    result = jnp.einsum(
        "wxyzbd,zabced->waxcey", real_form(matrix), shaped, precision=lax.Precision.HIGHEST
    )
    return result.reshape(2, -1)


def rotate(amps_now, theta):
    cosine = jnp.cos(theta)
    sine = jnp.sin(theta)
    return jnp.stack(
        (cosine * amps_now[0] - sine * amps_now[1], sine * amps_now[0] + cosine * amps_now[1])
    )


def bit_of(index_all, qubit):
    return jnp.bitwise_and(jnp.right_shift(index_all, qubit), 1)


def located(qubit, first_open, global_count, local_bits):
    moved_up = (qubit >= 7 + first_open) & (qubit < 7 + global_count)
    moved_down = (qubit >= local_bits + first_open) & (qubit < local_bits + global_count)
    return jnp.where(
        moved_up, qubit - 7 + local_bits, jnp.where(moved_down, qubit - local_bits + 7, qubit)
    )


def enter_qubit(amps_now, bit_number, local_bits, device_place):
    shaped = amps_now.reshape(2, 2 ** (local_bits - 8 - bit_number), 2, 2**bit_number, 128)
    zero_half = shaped[:, :, 0]
    one_half = shaped[:, :, 1]
    upper_side = jnp.bitwise_and(jnp.right_shift(device_place, bit_number), 1) == 1
    kept_half = jnp.where(upper_side, one_half, zero_half)
    sent_half = jnp.where(upper_side, zero_half, one_half)
    came_half = from_partner(sent_half, "hi", bit_number)
    new_zero = jnp.where(upper_side, came_half, kept_half)
    new_one = jnp.where(upper_side, kept_half, came_half)
    return jnp.stack((new_zero, new_one), axis=2).reshape(2, -1)


def shards(
    amplitudes, gate_matrices, phase_qubits, phase_angles, cut_qubits, cut_angle, path_index
):
    global_count = lax.axis_size("hi").bit_length() - 1
    amp_count = amplitudes.shape[1]
    local_bits = amp_count.bit_length() - 1
    device_place = lax.axis_index("hi")
    index_all = device_place * amp_count + lax.iota(jnp.int32, amp_count)
    layer_count = gate_matrices.shape[0]
    result = amplitudes
    for layer_number in range(layer_count):
        if layer_number < global_count:
            result = enter_qubit(result, layer_number, local_bits, device_place)
            target = 7 + layer_number
        else:
            if layer_number == global_count:
                shaped = result.reshape(2, 2**global_count, 2 ** (local_bits - global_count))
                result = lax.all_to_all(
                    shaped, "hi", split_axis=1, concat_axis=1, tiled=True
                ).reshape(2, -1)
            target = local_bits - 2 * global_count + layer_number
        result = apply_gate(result, gate_matrices[layer_number], target, local_bits)
        theta = jnp.zeros((amp_count,), jnp.float32)
        for pair_number in range(phase_qubits.shape[1]):
            first_pos = located(
                phase_qubits[layer_number, pair_number, 0], global_count, global_count, local_bits
            )
            second_pos = located(
                phase_qubits[layer_number, pair_number, 1], global_count, global_count, local_bits
            )
            both_bits = bit_of(index_all, first_pos) * bit_of(index_all, second_pos)
            theta = theta + phase_angles[layer_number, pair_number] * both_bits.astype(jnp.float32)
        result = rotate(result, theta)
        if layer_number == 0:
            for cut_number in range(cut_qubits.shape[0]):
                first_cut = located(
                    cut_qubits[cut_number, 0], global_count, global_count, local_bits
                )
                second_cut = located(
                    cut_qubits[cut_number, 1], global_count, global_count, local_bits
                )
                parity = jnp.bitwise_xor(
                    bit_of(index_all, first_cut), bit_of(index_all, second_cut)
                )
                signs = (1 - 2 * parity).astype(jnp.float32)
                chosen = path_index[cut_number] == 0
                angle_now = cut_angle[cut_number]
                keep_part = jnp.where(chosen, jnp.cos(angle_now), jnp.zeros_like(angle_now))
                turn_part = jnp.where(chosen, jnp.zeros_like(angle_now), jnp.sin(angle_now))
                result = jnp.stack(
                    (
                        keep_part * result[0] + turn_part * signs * result[1],
                        keep_part * result[1] - turn_part * signs * result[0],
                    )
                )
    return result


def any_slice(amplitudes, gate_matrices, *rest):
    g = lax.axis_size("hi").bit_length() - 1
    local_bits = amplitudes.shape[1].bit_length() - 1
    late_layers = gate_matrices.shape[0] - g
    fits = 3 <= g <= local_bits - g - 7 and local_bits - g >= 11 and 0 < late_layers <= 3
    plan = one_exchange if fits else shards
    return plan(amplitudes, gate_matrices, *rest)


def solution(mesh):
    placed = (
        P(None, ("paths", "hi")),
        P(),
        P("paths", None, None),
        P("paths", None),
        P("paths", None),
        P("paths"),
        P("paths"),
    )
    return jax.shard_map(
        any_slice, mesh=mesh, in_specs=placed, out_specs=P(None, ("paths", "hi")), check_vma=False
    )
```

```python
import functools
import math

import jax
import jax.numpy as jnp
from jax import lax
from jax.experimental import pallas as pl
from jax.experimental.pallas import tpu as pltpu
from jax.sharding import PartitionSpec as P

LANES = 128
SUB = 8
MESH = pl.DeviceIdType.MESH


def quarter_sincos(turns):
    whole = jnp.floor(turns + 0.5)
    rest = turns - whole
    square = rest * rest
    half_pi = math.pi / 2
    sin_terms = [(-1) ** k * half_pi ** (2 * k + 1) / math.factorial(2 * k + 1) for k in range(5)]
    cos_terms = [(-1) ** k * half_pi ** (2 * k) / math.factorial(2 * k) for k in range(6)]
    sine = jnp.full_like(square, sin_terms[-1])
    for term in sin_terms[-2::-1]:
        sine = sine * square + term
    sine = sine * rest
    cosine = jnp.full_like(square, cos_terms[-1])
    for term in cos_terms[-2::-1]:
        cosine = cosine * square + term
    count = whole.astype(jnp.int32)
    odd = (count & 1) == 1
    sin_out = jnp.where(odd, cosine, sine)
    cos_out = jnp.where(odd, sine, cosine)
    sin_out = jnp.where((count & 2) == 2, -sin_out, sin_out)
    cos_out = jnp.where(((count + 1) & 2) == 2, -cos_out, cos_out)
    return sin_out, cos_out


def swap_half(value):
    return pltpu.roll(value, LANES // 2, axis=1)


def spread(value, moves):
    total = None
    for a, b in moves:
        term = ((value >> a) & 1) << b
        total = term if total is None else total + term
    return total


def times(a, b):
    return a[0] * b[0] - a[1] * b[1], a[0] * b[1] + a[1] * b[0]


def circuit_kernel(
    g, local_bits, layers, pairs, cuts,
    amp_ref, gate_ref, qubit_in, angle_in, cut_qubit_in, cut_angle_in, path_in, out_ref,
    qubit_ref, angle_ref, cut_qubit_ref, cut_angle_ref, path_ref,
    recv, weights, gates, cos_all, sin_all, x_tab, y_tab, r_tab, mixed, turned,
    relay_in, relay_out, cos_far, sin_far,
    send_sem, recv_sem, relay_sem, gate_sem, small_sem, came_sem, go_sem,
):
    n = 2**g
    half, quarter = n // 2, n // 4
    block_bits = local_bits - g - 7
    chunks = 2 ** (block_bits - 3)
    piece = 2 * SUB
    rows = n * SUB
    half_rows = half * SUB
    early = chunks // 2
    late = list(range(early, chunks))
    last = chunks - 1
    me = lax.axis_index("hi")
    top = me // half
    spot = lax.rem(me, half)
    mirror = (1 - top) * half + lax.rem(spot + top * quarter, half)

    def block_rows(owner, chunk):
        return pl.ds(pl.multiple_of((owner * chunks + chunk) * piece, piece), piece)

    def slot_rows(source):
        return pl.ds(pl.multiple_of(source * piece, piece), piece)

    def half_slots(side):
        return pl.ds(pl.multiple_of(side * half * piece, half * piece), half * piece)

    def send(chunk, peer):
        pltpu.make_async_remote_copy(
            src_ref=amp_ref.at[block_rows(peer, chunk)],
            dst_ref=recv.at[chunk, slot_rows(me)],
            send_sem=send_sem.at[chunk],
            recv_sem=recv_sem.at[chunk, top],
            device_id={"hi": peer},
            device_id_type=MESH,
        ).start()

    def arrived(chunk, side):
        here = recv.at[chunk, half_slots(side)]
        pltpu.make_async_copy(here, here, recv_sem.at[chunk, side]).wait()

    def relay_piece(off):
        target = relay_in.at[pl.ds(pl.multiple_of(spot * piece, piece), piece)]
        if off == 0:
            return pltpu.make_async_copy(
                amp_ref.at[block_rows(mirror, last)], target, relay_sem.at[0]
            )
        peer = lax.rem(spot + off, half)
        return pltpu.make_async_remote_copy(
            src_ref=amp_ref.at[
                block_rows((1 - top) * half + lax.rem(peer + top * quarter, half), last)
            ],
            dst_ref=target,
            send_sem=send_sem.at[last],
            recv_sem=relay_sem.at[0],
            device_id={"hi": top * half + peer},
            device_id_type=MESH,
        )

    def send_relays():
        for off in range(half):
            relay_piece(off).start()

    def relay_result(c):
        mine = pl.ds(pl.multiple_of(top * half_rows, half_rows), half_rows)
        return pltpu.make_async_remote_copy(
            src_ref=relay_out.at[c],
            dst_ref=mixed.at[last, c, mine],
            send_sem=relay_sem.at[1],
            recv_sem=relay_sem.at[2],
            device_id={"hi": mirror},
            device_id_type=MESH,
        )

    def signal(semaphore, peer):
        pl.semaphore_signal(semaphore, inc=1, device_id={"hi": peer}, device_id_type=MESH)

    barrier = pltpu.get_barrier_semaphore()

    @pl.when(top == 0)
    def _():
        for off in range(half):
            signal(barrier, half + lax.rem(spot + off, half))
        for off in range(1, half):
            signal(barrier, lax.rem(spot + off, half))

    smalls = (
        (qubit_in, qubit_ref),
        (angle_in, angle_ref),
        (cut_qubit_in, cut_qubit_ref),
        (cut_angle_in, cut_angle_ref),
        (path_in, path_ref),
    )
    small_copies = [
        pltpu.make_async_copy(source, target, small_sem.at[k])
        for k, (source, target) in enumerate(smalls)
    ]
    for small_copy in small_copies:
        small_copy.start()
    gate_copy = pltpu.make_async_copy(gate_ref, gates, gate_sem)
    gate_copy.start()

    @pl.loop(0, chunks)
    def _(chunk):
        pltpu.make_async_copy(
            amp_ref.at[block_rows(me, chunk)],
            recv.at[chunk, slot_rows(me)],
            recv_sem.at[chunk, top],
        ).start()

    def send_near(first, last):
        @pl.loop(first, last)
        def _(chunk):
            for off in range(1, half):
                send(chunk, top * half + lax.rem(spot + off, half))

    def across_chips():
        for level in range(2):
            for off in range(quarter // 2):
                yield level * (quarter // 2) + lax.rem(spot // 2 + off, quarter // 2)

    def send_chip(chunk, chip):
        for off in range(2):
            send(chunk, (1 - top) * half + chip * 2 + lax.rem(spot + off, 2))

    @pl.when(top == 1)
    def _():
        pl.semaphore_wait(barrier, half)
        for off in range(half):
            signal(came_sem.at[spot // 2], half - 1 - off)

        @pl.loop(0, last)
        def _(chunk):
            for peer in range(0, half, 2):
                for core in range(2):
                    send(chunk, peer + lax.rem(spot + core, 2))

    low_lanes = lax.broadcasted_iota(jnp.int32, (64, LANES), 1) < 64
    blank = jnp.zeros((64, LANES), jnp.float32)

    def make_weights(layer):
        flat = [gates[layer, part].astype(jnp.float32).T for part in range(2)]
        for t in range(2):
            plain = [part[t * 64 : (t + 1) * 64] for part in flat]
            turned_part = [swap_half(part) for part in plain]
            for c in range(2):
                for t_out in range(2):
                    for c_out in range(2):
                        low_from, high_from = (
                            (plain, turned_part) if t_out == 0 else (turned_part, plain)
                        )
                        part = c ^ c_out
                        upper = jnp.where(low_lanes, low_from[part], blank)
                        lower = jnp.where(low_lanes, blank, high_from[part])
                        if c == 1 and c_out == 0:
                            upper, lower = -upper, -lower
                        block = jnp.concatenate((upper, lower), axis=0).astype(jnp.bfloat16)
                        row, column = (2 * t + c) * LANES, (2 * t_out + c_out) * LANES
                        weights[layer, row : row + LANES, column : column + LANES] = block

    def chunk_row(k):
        return block_bits + 3 + k if 10 + k < 7 + g else 3 + k

    lane = lax.broadcasted_iota(jnp.int32, (SUB, LANES), 1)
    sub = lax.broadcasted_iota(jnp.int32, (SUB, LANES), 0)
    to_quarter = 2.0 / math.pi
    chunk_places = [10 + k for k in range(block_bits - 3)]

    def entered(layer, q):
        if layer < g:
            up = (q >= 7) & (q <= 7 + layer)
            down = (q >= local_bits) & (q <= local_bits + layer)
            moved = local_bits - 7
            return q + jnp.where(up, moved, 0) - jnp.where(down, moved, 0)
        shift = jnp.where(q >= 7, local_bits - 7, 0)
        shift = jnp.where(q >= 7 + g, 0, shift)
        shift = jnp.where(q >= local_bits - g, 7 + g - local_bits, shift)
        shift = jnp.where(q >= local_bits, -g, shift)
        return q + shift

    def make_table(layer, owner, far=False):
        if layer < g:
            tile_places = [7, 8, 9]
            row_places = [local_bits + k for k in range(g)]
        else:
            tile_places = [local_bits + k for k in range(3)]
            row_places = [local_bits + k for k in range(3, g)] + [7, 8, 9]
        places = row_places + chunk_places
        masks, angles = [], []
        for k in range(pairs):
            masks.append(
                (jnp.int32(1) << entered(layer, qubit_ref[layer, 0, k]))
                | (jnp.int32(1) << entered(layer, qubit_ref[layer, 1, k]))
            )
            angles.append(angle_ref[layer, k] * to_quarter)

        def total(index, pick):
            turns = jnp.zeros((SUB, LANES), jnp.float32)
            for k in range(pairs):
                mask, angle = pick(masks[k], angles[k])
                turns = turns + jnp.where((index & mask) == mask, angle, 0.0)
            return turns

        tile_index = (
            lane
            + spread(sub, list(enumerate(tile_places)))
            + spread(owner, [(k, local_bits - g + k) for k in range(g)])
        )
        turns = [total(tile_index, lambda mask, angle: (mask, angle))]
        for place in places:
            bit = 1 << place
            turns.append(
                total(
                    tile_index | bit,
                    lambda mask, angle: (
                        mask, jnp.where(((mask & bit) != 0) & (mask != bit), angle, 0.0)
                    ),
                )
            )
        row_tiles = 2 ** len(places) // SUB
        for tile in range(row_tiles):
            row_index = spread(sub, list(enumerate(places[:3]))) + sum(
                (1 << place) if (tile >> k) & 1 else 0 for k, place in enumerate(places[3:])
            )
            turns.append(total(row_index, lambda mask, angle: (mask, angle)))
        if layer == 0:
            cut_mask = jnp.int32(0)
            cut_turns = jnp.float32(0)
            cut_size = jnp.full((SUB, LANES), 1.0, jnp.float32)
            for k in range(cuts):
                kept = path_ref[k] == 0
                bits = (jnp.int32(1) << entered(0, cut_qubit_ref[0, k])) ^ (
                    jnp.int32(1) << entered(0, cut_qubit_ref[1, k])
                )
                cut_mask = cut_mask ^ jnp.where(kept, 0, bits)
                cut_turns = cut_turns - jnp.where(kept, 0.0, 1.0)
                sine, cosine = quarter_sincos(
                    jnp.full((SUB, LANES), cut_angle_ref[k], jnp.float32) * to_quarter
                )
                kept_all = jnp.full((SUB, LANES), path_ref[k], jnp.int32) == 0
                cut_size = cut_size * jnp.where(kept_all, cosine, sine)
            folded = tile_index & cut_mask
            for shift in (16, 8, 4, 2, 1):
                folded = folded ^ (folded >> shift)
            turns[0] = turns[0] + cut_turns + ((folded & 1) * 2).astype(jnp.float32)
            for k, place in enumerate(places):
                turns[1 + k] = turns[1 + k] + jnp.where((cut_mask & (1 << place)) != 0, 2.0, 0.0)
        sine, cosine = quarter_sincos(jnp.stack(turns))
        waves = [(cosine[k], sine[k]) for k in range(len(turns))]
        base, steps, row_waves = waves[0], waves[1 : 1 + len(places)], waves[1 + len(places) :]
        if layer == 0:
            base = (base[0] * cut_size, base[1] * cut_size)
        for tile in range(row_tiles):
            for part in range(2):
                r_tab[layer, part, tile * SUB : (tile + 1) * SUB] = row_waves[tile][part]
        x_waves = [base]
        for step in steps[:3]:
            x_waves = x_waves + [times(wave, step) for wave in x_waves]
        y_waves = [None]
        for step in steps[3:]:
            y_waves = y_waves + [
                step if wave is None else times(wave, step) for wave in y_waves
            ]
        y_waves[0] = (jnp.ones((SUB, LANES), jnp.float32), jnp.zeros((SUB, LANES), jnp.float32))
        for tab, values in ((x_tab, x_waves), (y_tab, y_waves)):
            for k, wave in enumerate(values):
                for part in range(2):
                    tab[layer, k, part] = wave[part]
        per_chunk = n // SUB

        def entry(y, x):
            row = pl.ds(y * SUB + x, 1)
            row_wave = tuple(
                jnp.broadcast_to(r_tab[layer, part, row, :], (SUB, LANES)) for part in range(2)
            )
            x_wave = (x_tab[layer, x, 0], x_tab[layer, x, 1])
            y_wave = (y_tab[layer, y, 0], y_tab[layer, y, 1])
            return times(times(x_wave, y_wave), row_wave)

        if far:
            for tile in range(half // SUB):
                for x in range(SUB):
                    at = pl.ds(pl.multiple_of((tile * SUB + x) * SUB, SUB), SUB)
                    y = last * per_chunk + top * (half // SUB) + tile
                    cosine, sine = entry(y, x)
                    cos_far[layer, at] = cosine
                    sin_far[layer, at] = sine
            return

        @pl.loop(0, row_tiles)
        def _(y):
            chunk = y // per_chunk
            start = lax.rem(y, per_chunk) * (SUB * SUB)
            for x in range(SUB):
                at = pl.ds(pl.multiple_of(start + x * SUB, SUB), SUB)
                cosine, sine = entry(y, x)
                cos_all[layer, chunk, at] = cosine
                sin_all[layer, chunk, at] = sine

    def layer_step(state, layer, outer, inner, cosine, sine):
        count = outer * inner

        def pieces(value):
            shaped = value.reshape(outer, 2, inner, LANES)
            return [shaped[:, t].reshape(count, LANES) for t in range(2)]

        def whole(parts):
            shaped = [part.reshape(outer, inner, LANES) for part in parts]
            return jnp.stack(shaped, axis=1).reshape(2 * count, LANES)

        real, imag = pieces(state[0]), pieces(state[1])
        joined = jnp.concatenate((real[0], imag[0], real[1], imag[1]), axis=1)
        high = joined.astype(jnp.bfloat16)
        rest = (joined - high.astype(jnp.float32)).astype(jnp.bfloat16)
        both = jnp.dot(
            jnp.concatenate((high, rest), axis=0),
            weights[layer],
            preferred_element_type=jnp.float32,
        )
        product = both[:count] + both[count:]
        columns = [product[:, k * LANES : (k + 1) * LANES] for k in range(4)]
        return times((whole(columns[0::2]), whole(columns[1::2])), (cosine, sine))

    def half_layers(reads, tables):
        states = [tuple(read(c) for c in range(2)) for read in reads]
        for layer in range(g - 1):
            for k, table in enumerate(tables):
                cosine, sine = table(layer)
                outer = states[k][0].shape[0] // (2 ** (layer + 1) * SUB)
                states[k] = layer_step(states[k], layer, outer, 2**layer * SUB, cosine, sine)
        return states

    def first_layers(batches, side):
        start = pl.multiple_of(side * half * piece, half * piece)
        mine = pl.ds(pl.multiple_of(side * half_rows, half_rows), half_rows)

        def read(batch, c):
            part = pl.ds(start + c, half_rows, stride=2)
            return jnp.concatenate([recv[chunk, part, :] for chunk in batch], axis=0)

        def table(batch, layer):
            return tuple(
                jnp.concatenate([values[layer, chunk, mine] for chunk in batch], axis=0)
                for values in (cos_all, sin_all)
            )

        states = half_layers(
            [functools.partial(read, batch) for batch in batches],
            [functools.partial(table, batch) for batch in batches],
        )
        for state, batch in zip(states, batches):
            for k, chunk in enumerate(batch):
                for c in range(2):
                    mixed[chunk, c, mine] = state[c][k * half_rows : (k + 1) * half_rows]

    def relay_layers():
        states = half_layers(
            [lambda c: relay_in[pl.ds(c, half_rows, stride=2), :]],
            [lambda layer: (cos_far[layer], sin_far[layer])],
        )
        for c in range(2):
            relay_out[c] = states[0][c]

    def last_layers(batches):
        def whole_step(batch, state, layer, outer, inner):
            cosine, sine = (
                jnp.concatenate([table[layer, chunk] for chunk in batch], axis=0)
                for table in (cos_all, sin_all)
            )
            return layer_step(state, layer, len(batch) * outer, inner, cosine, sine)

        states = []
        for batch in batches:
            state = tuple(
                jnp.concatenate([mixed[chunk, c] for chunk in batch], axis=0) for c in range(2)
            )
            state = whole_step(batch, state, g - 1, 1, half * SUB)
            for c in range(2):
                for k, chunk in enumerate(batch):
                    turned[chunk, c] = state[c][k * rows : (k + 1) * rows]
            states.append(
                tuple(
                    jnp.concatenate(
                        [
                            turned[chunk, c, pl.ds(low, n, stride=SUB), :]
                            for chunk in batch
                            for low in range(SUB)
                        ],
                        axis=0,
                    )
                    for c in range(2)
                )
            )
        for layer in range(g, layers):
            k = layer - g
            for b, batch in enumerate(batches):
                states[b] = whole_step(batch, states[b], layer, 2 ** (2 - k), 2**k * n)
        for state, batch in zip(states, batches):
            for k, chunk in enumerate(batch):
                base = spread(chunk, [(k, chunk_row(k)) for k in range(block_bits - 3)])
                for low in range(SUB):
                    start = pl.multiple_of(2 * (base + (low << block_bits)), 2 * n)
                    for c in range(2):
                        out_ref[pl.ds(start + c, n, stride=2), :] = state[c][
                            k * rows + low * n : k * rows + (low + 1) * n
                        ]

    @pl.when(top == 0)
    def _():
        pl.semaphore_wait(barrier, half - 1)
        send_relays()

    for small_copy in small_copies:
        small_copy.wait()
    make_table(0, mirror, far=True)

    @pl.when(top == 0)
    def _():
        for chip in across_chips():
            pl.semaphore_wait(came_sem.at[chip], 2)
            send_chip(0, chip)

        @pl.when(spot >= quarter)
        def _():
            signal(go_sem, me + half)
            signal(go_sem, me + half - quarter)

        send_near(0, chunks)

        @pl.loop(1, last)
        def _(chunk):
            for chip in across_chips():
                send_chip(chunk, chip)

    for layer in range(1, g - 1):
        make_table(layer, mirror, far=True)
    gate_copy.wait()

    @pl.loop(0, layers)
    def _(layer):
        make_weights(layer)

    for layer in range(3):
        make_table(layer, me)

    @pl.when(top == 1)
    def _():
        pl.semaphore_wait(go_sem, 1)
        send_relays()
        send_near(0, chunks)

    for layer in range(3, layers):
        make_table(layer, me)

    pltpu.make_async_copy(relay_in, relay_in, relay_sem.at[0]).wait()
    relay_layers()
    for c in range(2):
        relay_result(c).start()

    for chunk in range(early):
        arrived(chunk, top)
    first_layers([[chunk] for chunk in range(early)], top)
    for chunk in range(early):
        arrived(chunk, 1 - top)
    first_layers([[chunk] for chunk in range(early)], 1 - top)
    last_layers([[chunk] for chunk in range(early)])

    for chunk in late:
        arrived(chunk, top)
    first_layers([[chunk] for chunk in late], top)
    for chunk in late[:-1]:
        arrived(chunk, 1 - top)
    first_layers([[chunk] for chunk in late[:-1]], 1 - top)
    came = recv.at[0, pl.ds(0, 2 * half_rows)]
    pltpu.make_async_copy(came, came, relay_sem.at[2]).wait()
    last_layers([[chunk] for chunk in late])

    def wait_sent(semaphore, count):
        gone = amp_ref.at[pl.ds(0, count)]
        pltpu.make_async_remote_copy(
            src_ref=gone,
            dst_ref=recv.at[0, pl.ds(0, count)],
            send_sem=semaphore,
            recv_sem=recv_sem.at[0, 0],
            device_id={"hi": lax.rem(me + 1, n)},
            device_id_type=MESH,
        ).wait_send()

    for chunk in range(last):
        wait_sent(send_sem.at[chunk], (n - 1) * piece)
    wait_sent(send_sem.at[last], (n - 2) * piece)
    wait_sent(relay_sem.at[1], 2 * half_rows)


def one_exchange(
    amplitudes, gate_matrices, phase_qubits, phase_angles, cut_qubits, cut_angle, path_index
):
    g = lax.axis_size("hi").bit_length() - 1
    amp_count = amplitudes.shape[1]
    local_bits = amp_count.bit_length() - 1
    layers, pairs = phase_angles.shape
    cuts = cut_angle.shape[0]
    n = 2**g
    chunks = 2 ** (local_bits - g - 10)
    rows = n * SUB
    all_rows = amp_count // LANES
    row_tiles = n * chunks // SUB
    whole = amplitudes.reshape(2, all_rows, LANES).transpose(1, 0, 2).reshape(2 * all_rows, LANES)
    hbm = pl.BlockSpec(memory_space=pltpu.HBM)
    result = pl.pallas_call(
        functools.partial(circuit_kernel, g, local_bits, layers, pairs, cuts),
        out_shape=pltpu.VMEM((2 * all_rows, LANES), jnp.float32),
        in_specs=[hbm] * 7,
        out_specs=pl.BlockSpec(memory_space=pltpu.VMEM),
        scratch_shapes=[
            pltpu.SMEM((layers, 2, pairs), jnp.int32),
            pltpu.SMEM(phase_angles.shape, jnp.float32),
            pltpu.SMEM((2, cuts), jnp.int32),
            pltpu.SMEM(cut_angle.shape, jnp.float32),
            pltpu.SMEM(path_index.shape, jnp.int32),
            pltpu.VMEM((chunks, 2 * rows, LANES), jnp.float32),
            pltpu.VMEM((layers, 512, 512), jnp.bfloat16),
            pltpu.VMEM(gate_matrices.shape, jnp.bfloat16),
            pltpu.VMEM((layers, chunks, rows, LANES), jnp.float32),
            pltpu.VMEM((layers, chunks, rows, LANES), jnp.float32),
            pltpu.VMEM((layers, SUB, 2, SUB, LANES), jnp.float32),
            pltpu.VMEM((layers, row_tiles, 2, SUB, LANES), jnp.float32),
            pltpu.VMEM((layers, 2, row_tiles * SUB, LANES), jnp.float32),
            pltpu.VMEM((chunks, 2, rows, LANES), jnp.float32),
            pltpu.VMEM((chunks, 2, rows, LANES), jnp.float32),
            pltpu.VMEM((rows, LANES), jnp.float32),
            pltpu.VMEM((2, rows // 2, LANES), jnp.float32),
            pltpu.VMEM((g - 1, rows // 2, LANES), jnp.float32),
            pltpu.VMEM((g - 1, rows // 2, LANES), jnp.float32),
            pltpu.SemaphoreType.DMA((chunks,)),
            pltpu.SemaphoreType.DMA((chunks, 2)),
            pltpu.SemaphoreType.DMA((3,)),
            pltpu.SemaphoreType.DMA,
            pltpu.SemaphoreType.DMA((5,)),
            pltpu.SemaphoreType.REGULAR((n // 4,)),
            pltpu.SemaphoreType.REGULAR,
        ],
        compiler_params=pltpu.CompilerParams(collective_id=0, has_side_effects=True),
    )(
        whole, gate_matrices, phase_qubits.transpose(0, 2, 1), phase_angles,
        cut_qubits.transpose(1, 0), cut_angle, path_index,
    )
    return result.reshape(all_rows, 2, LANES).transpose(1, 0, 2).reshape(2, amp_count)


def from_partner(value, axis, bit):
    return lax.ppermute(value, axis, [(i, i ^ 1 << bit) for i in range(lax.axis_size(axis))])


def real_form(matrix):
    real_part = matrix[0].astype(jnp.float32)
    imag_part = matrix[1].astype(jnp.float32)
    upper_rows = jnp.stack((real_part, -imag_part), axis=1)
    lower_rows = jnp.stack((imag_part, real_part), axis=1)
    stacked = jnp.stack((upper_rows, lower_rows), axis=0)
    return stacked.reshape(2, 2, 64, 2, 2, 64)


def apply_gate(amps_now, matrix, target, local_bits):
    shaped = amps_now.reshape(2, 2 ** (local_bits - 1 - target), 2, 2 ** (target - 7), 2, 64)
    result = jnp.einsum(
        "wxyzbd,zabced->waxcey", real_form(matrix), shaped, precision=lax.Precision.HIGHEST
    )
    return result.reshape(2, -1)


def rotate(amps_now, theta):
    cosine = jnp.cos(theta)
    sine = jnp.sin(theta)
    return jnp.stack(
        (cosine * amps_now[0] - sine * amps_now[1], sine * amps_now[0] + cosine * amps_now[1])
    )


def bit_of(index_all, qubit):
    return jnp.bitwise_and(jnp.right_shift(index_all, qubit), 1)


def located(qubit, first_open, global_count, local_bits):
    moved_up = (qubit >= 7 + first_open) & (qubit < 7 + global_count)
    moved_down = (qubit >= local_bits + first_open) & (qubit < local_bits + global_count)
    return jnp.where(
        moved_up, qubit - 7 + local_bits, jnp.where(moved_down, qubit - local_bits + 7, qubit)
    )


def enter_qubit(amps_now, bit_number, local_bits, device_place):
    shaped = amps_now.reshape(2, 2 ** (local_bits - 8 - bit_number), 2, 2**bit_number, 128)
    zero_half = shaped[:, :, 0]
    one_half = shaped[:, :, 1]
    upper_side = jnp.bitwise_and(jnp.right_shift(device_place, bit_number), 1) == 1
    kept_half = jnp.where(upper_side, one_half, zero_half)
    sent_half = jnp.where(upper_side, zero_half, one_half)
    came_half = from_partner(sent_half, "hi", bit_number)
    new_zero = jnp.where(upper_side, came_half, kept_half)
    new_one = jnp.where(upper_side, kept_half, came_half)
    return jnp.stack((new_zero, new_one), axis=2).reshape(2, -1)


def shards(
    amplitudes, gate_matrices, phase_qubits, phase_angles, cut_qubits, cut_angle, path_index
):
    global_count = lax.axis_size("hi").bit_length() - 1
    amp_count = amplitudes.shape[1]
    local_bits = amp_count.bit_length() - 1
    device_place = lax.axis_index("hi")
    index_all = device_place * amp_count + lax.iota(jnp.int32, amp_count)
    layer_count = gate_matrices.shape[0]
    result = amplitudes
    for layer_number in range(layer_count):
        if layer_number < global_count:
            result = enter_qubit(result, layer_number, local_bits, device_place)
            target = 7 + layer_number
        else:
            if layer_number == global_count:
                shaped = result.reshape(2, 2**global_count, 2 ** (local_bits - global_count))
                result = lax.all_to_all(
                    shaped, "hi", split_axis=1, concat_axis=1, tiled=True
                ).reshape(2, -1)
            target = local_bits - 2 * global_count + layer_number
        result = apply_gate(result, gate_matrices[layer_number], target, local_bits)
        theta = jnp.zeros((amp_count,), jnp.float32)
        for pair_number in range(phase_qubits.shape[1]):
            first_pos = located(
                phase_qubits[layer_number, pair_number, 0], global_count, global_count, local_bits
            )
            second_pos = located(
                phase_qubits[layer_number, pair_number, 1], global_count, global_count, local_bits
            )
            both_bits = bit_of(index_all, first_pos) * bit_of(index_all, second_pos)
            theta = theta + phase_angles[layer_number, pair_number] * both_bits.astype(jnp.float32)
        result = rotate(result, theta)
        if layer_number == 0:
            for cut_number in range(cut_qubits.shape[0]):
                first_cut = located(
                    cut_qubits[cut_number, 0], global_count, global_count, local_bits
                )
                second_cut = located(
                    cut_qubits[cut_number, 1], global_count, global_count, local_bits
                )
                parity = jnp.bitwise_xor(
                    bit_of(index_all, first_cut), bit_of(index_all, second_cut)
                )
                signs = (1 - 2 * parity).astype(jnp.float32)
                chosen = path_index[cut_number] == 0
                angle_now = cut_angle[cut_number]
                keep_part = jnp.where(chosen, jnp.cos(angle_now), jnp.zeros_like(angle_now))
                turn_part = jnp.where(chosen, jnp.zeros_like(angle_now), jnp.sin(angle_now))
                result = jnp.stack(
                    (
                        keep_part * result[0] + turn_part * signs * result[1],
                        keep_part * result[1] - turn_part * signs * result[0],
                    )
                )
    return result


def any_slice(amplitudes, gate_matrices, *rest):
    g = lax.axis_size("hi").bit_length() - 1
    local_bits = amplitudes.shape[1].bit_length() - 1
    late_layers = gate_matrices.shape[0] - g
    fits = 4 <= g <= local_bits - g - 7 and local_bits - g >= 12 and 0 < late_layers <= 3
    plan = one_exchange if fits else shards
    return plan(amplitudes, gate_matrices, *rest)


def solution(mesh):
    placed = (
        P(None, ("paths", "hi")),
        P(),
        P("paths", None, None),
        P("paths", None),
        P("paths", None),
        P("paths"),
        P("paths"),
    )
    return jax.shard_map(
        any_slice, mesh=mesh, in_specs=placed, out_specs=P(None, ("paths", "hi")), check_vma=False
    )
```

```python
import functools
import math

import jax
import jax.numpy as jnp
from jax import lax
from jax.experimental import pallas as pl
from jax.experimental.pallas import tpu as pltpu
from jax.sharding import PartitionSpec as P

LANES = 128
SUB = 8
MESH = pl.DeviceIdType.MESH


def quarter_sincos(turns):
    whole = jnp.floor(turns + 0.5)
    rest = turns - whole
    square = rest * rest
    half_pi = math.pi / 2
    sin_terms = [(-1) ** k * half_pi ** (2 * k + 1) / math.factorial(2 * k + 1) for k in range(5)]
    cos_terms = [(-1) ** k * half_pi ** (2 * k) / math.factorial(2 * k) for k in range(6)]
    sine = jnp.full_like(square, sin_terms[-1])
    for term in sin_terms[-2::-1]:
        sine = sine * square + term
    sine = sine * rest
    cosine = jnp.full_like(square, cos_terms[-1])
    for term in cos_terms[-2::-1]:
        cosine = cosine * square + term
    count = whole.astype(jnp.int32)
    odd = (count & 1) == 1
    sin_out = jnp.where(odd, cosine, sine)
    cos_out = jnp.where(odd, sine, cosine)
    sin_out = jnp.where((count & 2) == 2, -sin_out, sin_out)
    cos_out = jnp.where(((count + 1) & 2) == 2, -cos_out, cos_out)
    return sin_out, cos_out


def swap_half(value):
    return pltpu.roll(value, LANES // 2, axis=1)


def spread(value, moves):
    total = None
    for a, b in moves:
        term = ((value >> a) & 1) << b
        total = term if total is None else total + term
    return total


def times(a, b):
    return a[0] * b[0] - a[1] * b[1], a[0] * b[1] + a[1] * b[0]


def circuit_kernel(
    g, local_bits, layers, pairs, cuts,
    amp_ref, gate_ref, qubit_in, angle_in, cut_qubit_in, cut_angle_in, path_in, out_ref,
    qubit_ref, angle_ref, cut_qubit_ref, cut_angle_ref, path_ref,
    recv, weights, gates, cos_all, sin_all, x_tab, y_tab, r_tab, mixed, turned,
    relay_in, relay_out, cos_far, sin_far,
    send_sem, recv_sem, relay_sem, gate_sem, small_sem, came_sem, seen_sem, go_sem,
):
    n = 2**g
    half, quarter = n // 2, n // 4
    block_bits = local_bits - g - 7
    chunks = 2 ** (block_bits - 3)
    piece = 2 * SUB
    rows = n * SUB
    half_rows = half * SUB
    early = chunks // 2
    late = list(range(early, chunks))
    last = chunks - 1
    me = lax.axis_index("hi")
    top = me // half
    spot = lax.rem(me, half)
    columns = quarter // 2
    column = lax.rem(spot // 2, columns)
    mirror = (1 - top) * half + lax.rem(spot + top * quarter, half)

    def block_rows(owner, chunk):
        return pl.ds(pl.multiple_of((owner * chunks + chunk) * piece, piece), piece)

    def slot_rows(source):
        return pl.ds(pl.multiple_of(source * piece, piece), piece)

    def half_slots(side):
        return pl.ds(pl.multiple_of(side * half * piece, half * piece), half * piece)

    def send(chunk, peer):
        pltpu.make_async_remote_copy(
            src_ref=amp_ref.at[block_rows(peer, chunk)],
            dst_ref=recv.at[chunk, slot_rows(me)],
            send_sem=send_sem.at[chunk],
            recv_sem=recv_sem.at[chunk, top],
            device_id={"hi": peer},
            device_id_type=MESH,
        ).start()

    def arrived(chunk, side):
        here = recv.at[chunk, half_slots(side)]
        pltpu.make_async_copy(here, here, recv_sem.at[chunk, side]).wait()

    def relay_piece(off):
        target = relay_in.at[pl.ds(pl.multiple_of(spot * piece, piece), piece)]
        if off == 0:
            return pltpu.make_async_copy(
                amp_ref.at[block_rows(mirror, last)], target, relay_sem.at[0]
            )
        peer = lax.rem(spot + off, half)
        return pltpu.make_async_remote_copy(
            src_ref=amp_ref.at[
                block_rows((1 - top) * half + lax.rem(peer + top * quarter, half), last)
            ],
            dst_ref=target,
            send_sem=send_sem.at[last],
            recv_sem=relay_sem.at[0],
            device_id={"hi": top * half + peer},
            device_id_type=MESH,
        )

    def send_relays():
        for off in range(half):
            relay_piece(off).start()

    def relay_result(c):
        mine = pl.ds(pl.multiple_of(top * half_rows, half_rows), half_rows)
        return pltpu.make_async_remote_copy(
            src_ref=relay_out.at[c],
            dst_ref=mixed.at[last, c, mine],
            send_sem=relay_sem.at[1],
            recv_sem=relay_sem.at[2],
            device_id={"hi": mirror},
            device_id_type=MESH,
        )

    def signal(semaphore, peer):
        pl.semaphore_signal(semaphore, inc=1, device_id={"hi": peer}, device_id_type=MESH)

    barrier = pltpu.get_barrier_semaphore()

    @pl.when(top == 0)
    def _():
        for level in range(2):
            for core in range(2):
                signal(barrier, half + level * quarter + column * 2 + core)
        for off in range(1, half):
            signal(barrier, lax.rem(spot + off, half))

    smalls = (
        (qubit_in, qubit_ref),
        (angle_in, angle_ref),
        (cut_qubit_in, cut_qubit_ref),
        (cut_angle_in, cut_angle_ref),
        (path_in, path_ref),
    )
    small_copies = [
        pltpu.make_async_copy(source, target, small_sem.at[k])
        for k, (source, target) in enumerate(smalls)
    ]
    for small_copy in small_copies:
        small_copy.start()
    gate_copy = pltpu.make_async_copy(gate_ref, gates, gate_sem)
    gate_copy.start()

    @pl.loop(0, chunks)
    def _(chunk):
        pltpu.make_async_copy(
            amp_ref.at[block_rows(me, chunk)],
            recv.at[chunk, slot_rows(me)],
            recv_sem.at[chunk, top],
        ).start()

    def send_near(first, last):
        @pl.loop(first, last)
        def _(chunk):
            for off in range(1, half):
                send(chunk, top * half + lax.rem(spot + off, half))

    def send_column(chunk, level, off):
        there = (1 - top) * half + level * quarter + lax.rem(column + off, columns) * 2
        for core in range(2):
            send(chunk, there + lax.rem(spot + core, 2))

    def send_columns(first, offs):
        @pl.loop(first, last)
        def _(chunk):
            for level in range(2):
                for off in offs:
                    send_column(chunk, level, off)

    def send_levels(first, offs):
        for level in range(2):
            @pl.loop(first, last)
            def _(chunk):
                for off in offs:
                    send_column(chunk, level, off)

    @pl.when(top == 1)
    def _():
        pl.semaphore_wait(barrier, 4)
        for level in range(2):
            for core in range(2):
                signal(came_sem.at[spot // quarter], level * quarter + column * 2 + core)
        send_columns(0, [0])

    low_lanes = lax.broadcasted_iota(jnp.int32, (64, LANES), 1) < 64
    blank = jnp.zeros((64, LANES), jnp.float32)

    def make_weights(layer):
        flat = [gates[layer, part].astype(jnp.float32).T for part in range(2)]
        for t in range(2):
            plain = [part[t * 64 : (t + 1) * 64] for part in flat]
            turned_part = [swap_half(part) for part in plain]
            for c in range(2):
                for t_out in range(2):
                    for c_out in range(2):
                        low_from, high_from = (
                            (plain, turned_part) if t_out == 0 else (turned_part, plain)
                        )
                        part = c ^ c_out
                        upper = jnp.where(low_lanes, low_from[part], blank)
                        lower = jnp.where(low_lanes, blank, high_from[part])
                        if c == 1 and c_out == 0:
                            upper, lower = -upper, -lower
                        block = jnp.concatenate((upper, lower), axis=0).astype(jnp.bfloat16)
                        row, column = (2 * t + c) * LANES, (2 * t_out + c_out) * LANES
                        weights[layer, row : row + LANES, column : column + LANES] = block

    def chunk_row(k):
        return block_bits + 3 + k if 10 + k < 7 + g else 3 + k

    lane = lax.broadcasted_iota(jnp.int32, (SUB, LANES), 1)
    sub = lax.broadcasted_iota(jnp.int32, (SUB, LANES), 0)
    to_quarter = 2.0 / math.pi
    chunk_places = [10 + k for k in range(block_bits - 3)]

    def entered(layer, q):
        if layer < g:
            up = (q >= 7) & (q <= 7 + layer)
            down = (q >= local_bits) & (q <= local_bits + layer)
            moved = local_bits - 7
            return q + jnp.where(up, moved, 0) - jnp.where(down, moved, 0)
        shift = jnp.where(q >= 7, local_bits - 7, 0)
        shift = jnp.where(q >= 7 + g, 0, shift)
        shift = jnp.where(q >= local_bits - g, 7 + g - local_bits, shift)
        shift = jnp.where(q >= local_bits, -g, shift)
        return q + shift

    def make_table(layer, owner, far=False):
        if layer < g:
            tile_places = [7, 8, 9]
            row_places = [local_bits + k for k in range(g)]
        else:
            tile_places = [local_bits + k for k in range(3)]
            row_places = [local_bits + k for k in range(3, g)] + [7, 8, 9]
        places = row_places + chunk_places
        masks, angles = [], []
        for k in range(pairs):
            masks.append(
                (jnp.int32(1) << entered(layer, qubit_ref[layer, 0, k]))
                | (jnp.int32(1) << entered(layer, qubit_ref[layer, 1, k]))
            )
            angles.append(angle_ref[layer, k] * to_quarter)

        def total(index, pick):
            turns = jnp.zeros((SUB, LANES), jnp.float32)
            for k in range(pairs):
                mask, angle = pick(masks[k], angles[k])
                turns = turns + jnp.where((index & mask) == mask, angle, 0.0)
            return turns

        tile_index = (
            lane
            + spread(sub, list(enumerate(tile_places)))
            + spread(owner, [(k, local_bits - g + k) for k in range(g)])
        )
        turns = [total(tile_index, lambda mask, angle: (mask, angle))]
        for place in places:
            bit = 1 << place
            turns.append(
                total(
                    tile_index | bit,
                    lambda mask, angle: (
                        mask, jnp.where(((mask & bit) != 0) & (mask != bit), angle, 0.0)
                    ),
                )
            )
        row_tiles = 2 ** len(places) // SUB
        for tile in range(row_tiles):
            row_index = spread(sub, list(enumerate(places[:3]))) + sum(
                (1 << place) if (tile >> k) & 1 else 0 for k, place in enumerate(places[3:])
            )
            turns.append(total(row_index, lambda mask, angle: (mask, angle)))
        if layer == 0:
            cut_mask = jnp.int32(0)
            cut_turns = jnp.float32(0)
            cut_size = jnp.full((SUB, LANES), 1.0, jnp.float32)
            for k in range(cuts):
                kept = path_ref[k] == 0
                bits = (jnp.int32(1) << entered(0, cut_qubit_ref[0, k])) ^ (
                    jnp.int32(1) << entered(0, cut_qubit_ref[1, k])
                )
                cut_mask = cut_mask ^ jnp.where(kept, 0, bits)
                cut_turns = cut_turns - jnp.where(kept, 0.0, 1.0)
                sine, cosine = quarter_sincos(
                    jnp.full((SUB, LANES), cut_angle_ref[k], jnp.float32) * to_quarter
                )
                kept_all = jnp.full((SUB, LANES), path_ref[k], jnp.int32) == 0
                cut_size = cut_size * jnp.where(kept_all, cosine, sine)
            folded = tile_index & cut_mask
            for shift in (16, 8, 4, 2, 1):
                folded = folded ^ (folded >> shift)
            turns[0] = turns[0] + cut_turns + ((folded & 1) * 2).astype(jnp.float32)
            for k, place in enumerate(places):
                turns[1 + k] = turns[1 + k] + jnp.where((cut_mask & (1 << place)) != 0, 2.0, 0.0)
        sine, cosine = quarter_sincos(jnp.stack(turns))
        waves = [(cosine[k], sine[k]) for k in range(len(turns))]
        base, steps, row_waves = waves[0], waves[1 : 1 + len(places)], waves[1 + len(places) :]
        if layer == 0:
            base = (base[0] * cut_size, base[1] * cut_size)
        for tile in range(row_tiles):
            for part in range(2):
                r_tab[layer, part, tile * SUB : (tile + 1) * SUB] = row_waves[tile][part]
        x_waves = [base]
        for step in steps[:3]:
            x_waves = x_waves + [times(wave, step) for wave in x_waves]
        y_waves = [None]
        for step in steps[3:]:
            y_waves = y_waves + [
                step if wave is None else times(wave, step) for wave in y_waves
            ]
        y_waves[0] = (jnp.ones((SUB, LANES), jnp.float32), jnp.zeros((SUB, LANES), jnp.float32))
        for tab, values in ((x_tab, x_waves), (y_tab, y_waves)):
            for k, wave in enumerate(values):
                for part in range(2):
                    tab[layer, k, part] = wave[part]
        per_chunk = n // SUB

        def entry(y, x):
            row = pl.ds(y * SUB + x, 1)
            row_wave = tuple(
                jnp.broadcast_to(r_tab[layer, part, row, :], (SUB, LANES)) for part in range(2)
            )
            x_wave = (x_tab[layer, x, 0], x_tab[layer, x, 1])
            y_wave = (y_tab[layer, y, 0], y_tab[layer, y, 1])
            return times(times(x_wave, y_wave), row_wave)

        if far:
            for tile in range(half // SUB):
                for x in range(SUB):
                    at = pl.ds(pl.multiple_of((tile * SUB + x) * SUB, SUB), SUB)
                    y = last * per_chunk + top * (half // SUB) + tile
                    cosine, sine = entry(y, x)
                    cos_far[layer, at] = cosine
                    sin_far[layer, at] = sine
            return

        @pl.loop(0, row_tiles)
        def _(y):
            chunk = y // per_chunk
            start = lax.rem(y, per_chunk) * (SUB * SUB)
            for x in range(SUB):
                at = pl.ds(pl.multiple_of(start + x * SUB, SUB), SUB)
                cosine, sine = entry(y, x)
                cos_all[layer, chunk, at] = cosine
                sin_all[layer, chunk, at] = sine

    def layer_step(state, layer, outer, inner, cosine, sine):
        count = outer * inner

        def pieces(value):
            shaped = value.reshape(outer, 2, inner, LANES)
            return [shaped[:, t].reshape(count, LANES) for t in range(2)]

        def whole(parts):
            shaped = [part.reshape(outer, inner, LANES) for part in parts]
            return jnp.stack(shaped, axis=1).reshape(2 * count, LANES)

        real, imag = pieces(state[0]), pieces(state[1])
        joined = jnp.concatenate((real[0], imag[0], real[1], imag[1]), axis=1)
        high = joined.astype(jnp.bfloat16)
        rest = (joined - high.astype(jnp.float32)).astype(jnp.bfloat16)
        both = jnp.dot(
            jnp.concatenate((high, rest), axis=0),
            weights[layer],
            preferred_element_type=jnp.float32,
        )
        product = both[:count] + both[count:]
        columns = [product[:, k * LANES : (k + 1) * LANES] for k in range(4)]
        return times((whole(columns[0::2]), whole(columns[1::2])), (cosine, sine))

    def half_layers(reads, tables):
        states = [tuple(read(c) for c in range(2)) for read in reads]
        for layer in range(g - 1):
            for k, table in enumerate(tables):
                cosine, sine = table(layer)
                outer = states[k][0].shape[0] // (2 ** (layer + 1) * SUB)
                states[k] = layer_step(states[k], layer, outer, 2**layer * SUB, cosine, sine)
        return states

    def first_layers(batches, side):
        start = pl.multiple_of(side * half * piece, half * piece)
        mine = pl.ds(pl.multiple_of(side * half_rows, half_rows), half_rows)

        def read(batch, c):
            part = pl.ds(start + c, half_rows, stride=2)
            return jnp.concatenate([recv[chunk, part, :] for chunk in batch], axis=0)

        def table(batch, layer):
            return tuple(
                jnp.concatenate([values[layer, chunk, mine] for chunk in batch], axis=0)
                for values in (cos_all, sin_all)
            )

        states = half_layers(
            [functools.partial(read, batch) for batch in batches],
            [functools.partial(table, batch) for batch in batches],
        )
        for state, batch in zip(states, batches):
            for k, chunk in enumerate(batch):
                for c in range(2):
                    mixed[chunk, c, mine] = state[c][k * half_rows : (k + 1) * half_rows]

    def relay_layers():
        states = half_layers(
            [lambda c: relay_in[pl.ds(c, half_rows, stride=2), :]],
            [lambda layer: (cos_far[layer], sin_far[layer])],
        )
        for c in range(2):
            relay_out[c] = states[0][c]

    def last_layers(batches):
        def whole_step(batch, state, layer, outer, inner):
            cosine, sine = (
                jnp.concatenate([table[layer, chunk] for chunk in batch], axis=0)
                for table in (cos_all, sin_all)
            )
            return layer_step(state, layer, len(batch) * outer, inner, cosine, sine)

        states = []
        for batch in batches:
            state = tuple(
                jnp.concatenate([mixed[chunk, c] for chunk in batch], axis=0) for c in range(2)
            )
            state = whole_step(batch, state, g - 1, 1, half * SUB)
            for c in range(2):
                for k, chunk in enumerate(batch):
                    turned[chunk, c] = state[c][k * rows : (k + 1) * rows]
            states.append(
                tuple(
                    jnp.concatenate(
                        [
                            turned[chunk, c, pl.ds(low, n, stride=SUB), :]
                            for chunk in batch
                            for low in range(SUB)
                        ],
                        axis=0,
                    )
                    for c in range(2)
                )
            )
        for layer in range(g, layers):
            k = layer - g
            for b, batch in enumerate(batches):
                states[b] = whole_step(batch, states[b], layer, 2 ** (2 - k), 2**k * n)
        for state, batch in zip(states, batches):
            for k, chunk in enumerate(batch):
                base = spread(chunk, [(k, chunk_row(k)) for k in range(block_bits - 3)])
                for low in range(SUB):
                    start = pl.multiple_of(2 * (base + (low << block_bits)), 2 * n)
                    for c in range(2):
                        out_ref[pl.ds(start + c, n, stride=2), :] = state[c][
                            k * rows + low * n : k * rows + (low + 1) * n
                        ]

    @pl.when(top == 0)
    def _():
        pl.semaphore_wait(barrier, half - 1)
        send_relays()

    for small_copy in small_copies:
        small_copy.wait()
    make_table(0, mirror, far=True)

    @pl.when(top == 0)
    def _():
        for level in range(2):
            pl.semaphore_wait(came_sem.at[level], 2)
            send_column(0, level, 0)
        for off in range(1, columns):
            signal(seen_sem, me - column * 2 + lax.rem(column + off, columns) * 2)
        pl.semaphore_wait(seen_sem, columns - 1)

        @pl.when(spot >= quarter)
        def _():
            signal(go_sem, me + half)
            signal(go_sem, me + half - quarter)

        for level in range(2):
            for off in range(1, columns):
                send_column(0, level, off)
        send_near(0, chunks)
        send_columns(1, list(range(columns)))

    for layer in range(1, g - 1):
        make_table(layer, mirror, far=True)
    gate_copy.wait()

    @pl.loop(0, layers)
    def _(layer):
        make_weights(layer)

    for layer in range(1):
        make_table(layer, me)

    @pl.when(top == 1)
    def _():
        pl.semaphore_wait(go_sem, 1)
        send_relays()
        send_levels(0, list(range(1, columns)))
        send_near(0, early)

    for layer in range(1, layers):
        make_table(layer, me)

    pltpu.make_async_copy(relay_in, relay_in, relay_sem.at[0]).wait()
    relay_layers()
    for c in range(2):
        relay_result(c).start()

    @pl.when(top == 1)
    def _():
        send_near(early, chunks)

    for chunk in range(early):
        arrived(chunk, top)
    first_layers([[chunk] for chunk in range(early)], top)
    for chunk in range(early):
        arrived(chunk, 1 - top)
    first_layers([[chunk] for chunk in range(early)], 1 - top)
    last_layers([[chunk] for chunk in range(early)])

    for chunk in late:
        arrived(chunk, top)
    first_layers([[chunk] for chunk in late], top)
    for chunk in late[:-1]:
        arrived(chunk, 1 - top)
    first_layers([[chunk] for chunk in late[:-1]], 1 - top)
    came = recv.at[0, pl.ds(0, 2 * half_rows)]
    pltpu.make_async_copy(came, came, relay_sem.at[2]).wait()
    last_layers([[chunk] for chunk in late])

    def wait_sent(semaphore, count):
        gone = amp_ref.at[pl.ds(0, count)]
        pltpu.make_async_remote_copy(
            src_ref=gone,
            dst_ref=recv.at[0, pl.ds(0, count)],
            send_sem=semaphore,
            recv_sem=recv_sem.at[0, 0],
            device_id={"hi": lax.rem(me + 1, n)},
            device_id_type=MESH,
        ).wait_send()

    for chunk in range(last):
        wait_sent(send_sem.at[chunk], (n - 1) * piece)
    wait_sent(send_sem.at[last], (n - 2) * piece)
    wait_sent(relay_sem.at[1], 2 * half_rows)


def one_exchange(
    amplitudes, gate_matrices, phase_qubits, phase_angles, cut_qubits, cut_angle, path_index
):
    g = lax.axis_size("hi").bit_length() - 1
    amp_count = amplitudes.shape[1]
    local_bits = amp_count.bit_length() - 1
    layers, pairs = phase_angles.shape
    cuts = cut_angle.shape[0]
    n = 2**g
    chunks = 2 ** (local_bits - g - 10)
    rows = n * SUB
    all_rows = amp_count // LANES
    row_tiles = n * chunks // SUB
    whole = amplitudes.reshape(2, all_rows, LANES).transpose(1, 0, 2).reshape(2 * all_rows, LANES)
    hbm = pl.BlockSpec(memory_space=pltpu.HBM)
    result = pl.pallas_call(
        functools.partial(circuit_kernel, g, local_bits, layers, pairs, cuts),
        out_shape=pltpu.VMEM((2 * all_rows, LANES), jnp.float32),
        in_specs=[hbm] * 7,
        out_specs=pl.BlockSpec(memory_space=pltpu.VMEM),
        scratch_shapes=[
            pltpu.SMEM((layers, 2, pairs), jnp.int32),
            pltpu.SMEM(phase_angles.shape, jnp.float32),
            pltpu.SMEM((2, cuts), jnp.int32),
            pltpu.SMEM(cut_angle.shape, jnp.float32),
            pltpu.SMEM(path_index.shape, jnp.int32),
            pltpu.VMEM((chunks, 2 * rows, LANES), jnp.float32),
            pltpu.VMEM((layers, 512, 512), jnp.bfloat16),
            pltpu.VMEM(gate_matrices.shape, jnp.bfloat16),
            pltpu.VMEM((layers, chunks, rows, LANES), jnp.float32),
            pltpu.VMEM((layers, chunks, rows, LANES), jnp.float32),
            pltpu.VMEM((layers, SUB, 2, SUB, LANES), jnp.float32),
            pltpu.VMEM((layers, row_tiles, 2, SUB, LANES), jnp.float32),
            pltpu.VMEM((layers, 2, row_tiles * SUB, LANES), jnp.float32),
            pltpu.VMEM((chunks, 2, rows, LANES), jnp.float32),
            pltpu.VMEM((chunks, 2, rows, LANES), jnp.float32),
            pltpu.VMEM((rows, LANES), jnp.float32),
            pltpu.VMEM((2, rows // 2, LANES), jnp.float32),
            pltpu.VMEM((g - 1, rows // 2, LANES), jnp.float32),
            pltpu.VMEM((g - 1, rows // 2, LANES), jnp.float32),
            pltpu.SemaphoreType.DMA((chunks,)),
            pltpu.SemaphoreType.DMA((chunks, 2)),
            pltpu.SemaphoreType.DMA((3,)),
            pltpu.SemaphoreType.DMA,
            pltpu.SemaphoreType.DMA((5,)),
            pltpu.SemaphoreType.REGULAR((2,)),
            pltpu.SemaphoreType.REGULAR,
            pltpu.SemaphoreType.REGULAR,
        ],
        compiler_params=pltpu.CompilerParams(collective_id=0, has_side_effects=True),
    )(
        whole, gate_matrices, phase_qubits.transpose(0, 2, 1), phase_angles,
        cut_qubits.transpose(1, 0), cut_angle, path_index,
    )
    return result.reshape(all_rows, 2, LANES).transpose(1, 0, 2).reshape(2, amp_count)


def from_partner(value, axis, bit):
    return lax.ppermute(value, axis, [(i, i ^ 1 << bit) for i in range(lax.axis_size(axis))])


def real_form(matrix):
    real_part = matrix[0].astype(jnp.float32)
    imag_part = matrix[1].astype(jnp.float32)
    upper_rows = jnp.stack((real_part, -imag_part), axis=1)
    lower_rows = jnp.stack((imag_part, real_part), axis=1)
    stacked = jnp.stack((upper_rows, lower_rows), axis=0)
    return stacked.reshape(2, 2, 64, 2, 2, 64)


def apply_gate(amps_now, matrix, target, local_bits):
    shaped = amps_now.reshape(2, 2 ** (local_bits - 1 - target), 2, 2 ** (target - 7), 2, 64)
    result = jnp.einsum(
        "wxyzbd,zabced->waxcey", real_form(matrix), shaped, precision=lax.Precision.HIGHEST
    )
    return result.reshape(2, -1)


def rotate(amps_now, theta):
    cosine = jnp.cos(theta)
    sine = jnp.sin(theta)
    return jnp.stack(
        (cosine * amps_now[0] - sine * amps_now[1], sine * amps_now[0] + cosine * amps_now[1])
    )


def bit_of(index_all, qubit):
    return jnp.bitwise_and(jnp.right_shift(index_all, qubit), 1)


def located(qubit, first_open, global_count, local_bits):
    moved_up = (qubit >= 7 + first_open) & (qubit < 7 + global_count)
    moved_down = (qubit >= local_bits + first_open) & (qubit < local_bits + global_count)
    return jnp.where(
        moved_up, qubit - 7 + local_bits, jnp.where(moved_down, qubit - local_bits + 7, qubit)
    )


def enter_qubit(amps_now, bit_number, local_bits, device_place):
    shaped = amps_now.reshape(2, 2 ** (local_bits - 8 - bit_number), 2, 2**bit_number, 128)
    zero_half = shaped[:, :, 0]
    one_half = shaped[:, :, 1]
    upper_side = jnp.bitwise_and(jnp.right_shift(device_place, bit_number), 1) == 1
    kept_half = jnp.where(upper_side, one_half, zero_half)
    sent_half = jnp.where(upper_side, zero_half, one_half)
    came_half = from_partner(sent_half, "hi", bit_number)
    new_zero = jnp.where(upper_side, came_half, kept_half)
    new_one = jnp.where(upper_side, kept_half, came_half)
    return jnp.stack((new_zero, new_one), axis=2).reshape(2, -1)


def shards(
    amplitudes, gate_matrices, phase_qubits, phase_angles, cut_qubits, cut_angle, path_index
):
    global_count = lax.axis_size("hi").bit_length() - 1
    amp_count = amplitudes.shape[1]
    local_bits = amp_count.bit_length() - 1
    device_place = lax.axis_index("hi")
    index_all = device_place * amp_count + lax.iota(jnp.int32, amp_count)
    layer_count = gate_matrices.shape[0]
    result = amplitudes
    for layer_number in range(layer_count):
        if layer_number < global_count:
            result = enter_qubit(result, layer_number, local_bits, device_place)
            target = 7 + layer_number
        else:
            if layer_number == global_count:
                shaped = result.reshape(2, 2**global_count, 2 ** (local_bits - global_count))
                result = lax.all_to_all(
                    shaped, "hi", split_axis=1, concat_axis=1, tiled=True
                ).reshape(2, -1)
            target = local_bits - 2 * global_count + layer_number
        result = apply_gate(result, gate_matrices[layer_number], target, local_bits)
        theta = jnp.zeros((amp_count,), jnp.float32)
        for pair_number in range(phase_qubits.shape[1]):
            first_pos = located(
                phase_qubits[layer_number, pair_number, 0], global_count, global_count, local_bits
            )
            second_pos = located(
                phase_qubits[layer_number, pair_number, 1], global_count, global_count, local_bits
            )
            both_bits = bit_of(index_all, first_pos) * bit_of(index_all, second_pos)
            theta = theta + phase_angles[layer_number, pair_number] * both_bits.astype(jnp.float32)
        result = rotate(result, theta)
        if layer_number == 0:
            for cut_number in range(cut_qubits.shape[0]):
                first_cut = located(
                    cut_qubits[cut_number, 0], global_count, global_count, local_bits
                )
                second_cut = located(
                    cut_qubits[cut_number, 1], global_count, global_count, local_bits
                )
                parity = jnp.bitwise_xor(
                    bit_of(index_all, first_cut), bit_of(index_all, second_cut)
                )
                signs = (1 - 2 * parity).astype(jnp.float32)
                chosen = path_index[cut_number] == 0
                angle_now = cut_angle[cut_number]
                keep_part = jnp.where(chosen, jnp.cos(angle_now), jnp.zeros_like(angle_now))
                turn_part = jnp.where(chosen, jnp.zeros_like(angle_now), jnp.sin(angle_now))
                result = jnp.stack(
                    (
                        keep_part * result[0] + turn_part * signs * result[1],
                        keep_part * result[1] - turn_part * signs * result[0],
                    )
                )
    return result


def any_slice(amplitudes, gate_matrices, *rest):
    g = lax.axis_size("hi").bit_length() - 1
    local_bits = amplitudes.shape[1].bit_length() - 1
    late_layers = gate_matrices.shape[0] - g
    fits = 4 <= g <= local_bits - g - 7 and local_bits - g >= 12 and 0 < late_layers <= 3
    plan = one_exchange if fits else shards
    return plan(amplitudes, gate_matrices, *rest)


def solution(mesh):
    placed = (
        P(None, ("paths", "hi")),
        P(),
        P("paths", None, None),
        P("paths", None),
        P("paths", None),
        P("paths"),
        P("paths"),
    )
    return jax.shard_map(
        any_slice, mesh=mesh, in_specs=placed, out_specs=P(None, ("paths", "hi")), check_vma=False
    )
```

```python
import functools
import math

import jax
import jax.numpy as jnp
from jax import lax
from jax.experimental import pallas as pl
from jax.experimental.pallas import tpu as pltpu
from jax.sharding import PartitionSpec as P

LANES = 128
SUB = 8
MESH = pl.DeviceIdType.MESH


def quarter_sincos(turns):
    whole = jnp.floor(turns + 0.5)
    rest = turns - whole
    square = rest * rest
    half_pi = math.pi / 2
    sin_terms = [(-1) ** k * half_pi ** (2 * k + 1) / math.factorial(2 * k + 1) for k in range(5)]
    cos_terms = [(-1) ** k * half_pi ** (2 * k) / math.factorial(2 * k) for k in range(6)]
    sine = jnp.full_like(square, sin_terms[-1])
    for term in sin_terms[-2::-1]:
        sine = sine * square + term
    sine = sine * rest
    cosine = jnp.full_like(square, cos_terms[-1])
    for term in cos_terms[-2::-1]:
        cosine = cosine * square + term
    count = whole.astype(jnp.int32)
    odd = (count & 1) == 1
    sin_out = jnp.where(odd, cosine, sine)
    cos_out = jnp.where(odd, sine, cosine)
    sin_out = jnp.where((count & 2) == 2, -sin_out, sin_out)
    cos_out = jnp.where(((count + 1) & 2) == 2, -cos_out, cos_out)
    return sin_out, cos_out


def swap_half(value):
    return pltpu.roll(value, LANES // 2, axis=1)


def spread(value, moves):
    total = None
    for a, b in moves:
        term = ((value >> a) & 1) << b
        total = term if total is None else total + term
    return total


def times(a, b):
    return a[0] * b[0] - a[1] * b[1], a[0] * b[1] + a[1] * b[0]


def circuit_kernel(
    g, local_bits, layers, pairs, cuts,
    amp_ref, gate_ref, qubit_in, angle_in, cut_qubit_in, cut_angle_in, path_in, out_ref,
    qubit_ref, angle_ref, cut_qubit_ref, cut_angle_ref, path_ref,
    recv, weights, gates, cos_all, sin_all, x_tab, y_tab, r_tab, mixed, turned,
    relay_in, relay_out, cos_far, sin_far,
    send_sem, recv_sem, relay_sem, gate_sem, small_sem, came_sem, seen_sem, go_sem,
):
    n = 2**g
    half, quarter = n // 2, n // 4
    block_bits = local_bits - g - 7
    chunks = 2 ** (block_bits - 3)
    piece = 2 * SUB
    rows = n * SUB
    half_rows = half * SUB
    early = chunks // 2
    late = list(range(early, chunks))
    last = chunks - 1
    me = lax.axis_index("hi")
    top = me // half
    spot = lax.rem(me, half)
    columns = quarter // 2
    column = lax.rem(spot // 2, columns)
    mirror = (1 - top) * half + lax.rem(spot + top * quarter, half)

    def block_rows(owner, chunk):
        return pl.ds(pl.multiple_of((owner * chunks + chunk) * piece, piece), piece)

    def slot_rows(source):
        return pl.ds(pl.multiple_of(source * piece, piece), piece)

    def half_slots(side):
        return pl.ds(pl.multiple_of(side * half * piece, half * piece), half * piece)

    def send(chunk, peer):
        pltpu.make_async_remote_copy(
            src_ref=amp_ref.at[block_rows(peer, chunk)],
            dst_ref=recv.at[chunk, slot_rows(me)],
            send_sem=send_sem.at[chunk],
            recv_sem=recv_sem.at[chunk, top],
            device_id={"hi": peer},
            device_id_type=MESH,
        ).start()

    def arrived(chunk, side):
        here = recv.at[chunk, half_slots(side)]
        pltpu.make_async_copy(here, here, recv_sem.at[chunk, side]).wait()

    def relay_piece(off):
        target = relay_in.at[pl.ds(pl.multiple_of(spot * piece, piece), piece)]
        if off == 0:
            return pltpu.make_async_copy(
                amp_ref.at[block_rows(mirror, last)], target, relay_sem.at[0]
            )
        peer = lax.rem(spot + off, half)
        return pltpu.make_async_remote_copy(
            src_ref=amp_ref.at[
                block_rows((1 - top) * half + lax.rem(peer + top * quarter, half), last)
            ],
            dst_ref=target,
            send_sem=send_sem.at[last],
            recv_sem=relay_sem.at[0],
            device_id={"hi": top * half + peer},
            device_id_type=MESH,
        )

    def send_relays():
        for off in range(half):
            relay_piece(off).start()

    def relay_result(c):
        mine = pl.ds(pl.multiple_of(top * half_rows, half_rows), half_rows)
        return pltpu.make_async_remote_copy(
            src_ref=relay_out.at[c],
            dst_ref=mixed.at[last, c, mine],
            send_sem=relay_sem.at[1],
            recv_sem=relay_sem.at[2],
            device_id={"hi": mirror},
            device_id_type=MESH,
        )

    def signal(semaphore, peer):
        pl.semaphore_signal(semaphore, inc=1, device_id={"hi": peer}, device_id_type=MESH)

    barrier = pltpu.get_barrier_semaphore()

    @pl.when(top == 0)
    def _():
        for level in range(2):
            for core in range(2):
                signal(barrier, half + level * quarter + column * 2 + core)
        for off in range(1, half):
            signal(barrier, lax.rem(spot + off, half))

    smalls = (
        (qubit_in, qubit_ref),
        (angle_in, angle_ref),
        (cut_qubit_in, cut_qubit_ref),
        (cut_angle_in, cut_angle_ref),
        (path_in, path_ref),
    )
    small_copies = [
        pltpu.make_async_copy(source, target, small_sem.at[k])
        for k, (source, target) in enumerate(smalls)
    ]
    for small_copy in small_copies:
        small_copy.start()
    gate_copy = pltpu.make_async_copy(gate_ref, gates, gate_sem)
    gate_copy.start()

    @pl.loop(0, chunks)
    def _(chunk):
        pltpu.make_async_copy(
            amp_ref.at[block_rows(me, chunk)],
            recv.at[chunk, slot_rows(me)],
            recv_sem.at[chunk, top],
        ).start()

    def send_near(first, last):
        @pl.loop(first, last)
        def _(chunk):
            for off in range(1, half):
                send(chunk, top * half + lax.rem(spot + off, half))

    def send_column(chunk, level, off):
        there = (1 - top) * half + level * quarter + lax.rem(column + off, columns) * 2
        for core in range(2):
            send(chunk, there + lax.rem(spot + core, 2))

    def send_columns(first, offs):
        @pl.loop(first, last)
        def _(chunk):
            for level in range(2):
                for off in offs:
                    send_column(chunk, level, off)

    def send_levels(first, offs):
        for level in range(2):
            @pl.loop(first, last)
            def _(chunk):
                for off in offs:
                    send_column(chunk, level, off)

    @pl.when(top == 1)
    def _():
        pl.semaphore_wait(barrier, 4)
        for level in range(2):
            for core in range(2):
                signal(came_sem.at[spot // quarter], level * quarter + column * 2 + core)
        send_columns(0, [0])

    low_lanes = lax.broadcasted_iota(jnp.int32, (64, LANES), 1) < 64
    blank = jnp.zeros((64, LANES), jnp.float32)

    def make_weights(layer):
        flat = [gates[layer, part].astype(jnp.float32).T for part in range(2)]
        for t in range(2):
            plain = [part[t * 64 : (t + 1) * 64] for part in flat]
            turned_part = [swap_half(part) for part in plain]
            for c in range(2):
                for t_out in range(2):
                    for c_out in range(2):
                        low_from, high_from = (
                            (plain, turned_part) if t_out == 0 else (turned_part, plain)
                        )
                        part = c ^ c_out
                        upper = jnp.where(low_lanes, low_from[part], blank)
                        lower = jnp.where(low_lanes, blank, high_from[part])
                        if c == 1 and c_out == 0:
                            upper, lower = -upper, -lower
                        block = jnp.concatenate((upper, lower), axis=0).astype(jnp.bfloat16)
                        row, column = (2 * t + c) * LANES, (2 * t_out + c_out) * LANES
                        weights[layer, row : row + LANES, column : column + LANES] = block

    def chunk_row(k):
        return block_bits + 3 + k if 10 + k < 7 + g else 3 + k

    lane = lax.broadcasted_iota(jnp.int32, (SUB, LANES), 1)
    sub = lax.broadcasted_iota(jnp.int32, (SUB, LANES), 0)
    to_quarter = 2.0 / math.pi
    chunk_places = [10 + k for k in range(block_bits - 3)]

    def entered(layer, q):
        if layer < g:
            up = (q >= 7) & (q <= 7 + layer)
            down = (q >= local_bits) & (q <= local_bits + layer)
            moved = local_bits - 7
            return q + jnp.where(up, moved, 0) - jnp.where(down, moved, 0)
        shift = jnp.where(q >= 7, local_bits - 7, 0)
        shift = jnp.where(q >= 7 + g, 0, shift)
        shift = jnp.where(q >= local_bits - g, 7 + g - local_bits, shift)
        shift = jnp.where(q >= local_bits, -g, shift)
        return q + shift

    def make_table(layer, owner, far=False):
        if layer < g:
            tile_places = [7, 8, 9]
            row_places = [local_bits + k for k in range(g)]
        else:
            tile_places = [local_bits + k for k in range(3)]
            row_places = [local_bits + k for k in range(3, g)] + [7, 8, 9]
        places = row_places + chunk_places
        masks, angles = [], []
        for k in range(pairs):
            masks.append(
                (jnp.int32(1) << entered(layer, qubit_ref[layer, 0, k]))
                | (jnp.int32(1) << entered(layer, qubit_ref[layer, 1, k]))
            )
            angles.append(angle_ref[layer, k] * to_quarter)

        def total(index, pick):
            turns = jnp.zeros((SUB, LANES), jnp.float32)
            for k in range(pairs):
                mask, angle = pick(masks[k], angles[k])
                turns = turns + jnp.where((index & mask) == mask, angle, 0.0)
            return turns

        tile_index = (
            lane
            + spread(sub, list(enumerate(tile_places)))
            + spread(owner, [(k, local_bits - g + k) for k in range(g)])
        )
        turns = [total(tile_index, lambda mask, angle: (mask, angle))]
        for place in places:
            bit = 1 << place
            turns.append(
                total(
                    tile_index | bit,
                    lambda mask, angle: (
                        mask, jnp.where(((mask & bit) != 0) & (mask != bit), angle, 0.0)
                    ),
                )
            )
        row_tiles = 2 ** len(places) // SUB
        for tile in range(row_tiles):
            row_index = spread(sub, list(enumerate(places[:3]))) + sum(
                (1 << place) if (tile >> k) & 1 else 0 for k, place in enumerate(places[3:])
            )
            turns.append(total(row_index, lambda mask, angle: (mask, angle)))
        if layer == 0:
            cut_mask = jnp.int32(0)
            cut_turns = jnp.float32(0)
            cut_size = jnp.full((SUB, LANES), 1.0, jnp.float32)
            for k in range(cuts):
                kept = path_ref[k] == 0
                bits = (jnp.int32(1) << entered(0, cut_qubit_ref[0, k])) ^ (
                    jnp.int32(1) << entered(0, cut_qubit_ref[1, k])
                )
                cut_mask = cut_mask ^ jnp.where(kept, 0, bits)
                cut_turns = cut_turns - jnp.where(kept, 0.0, 1.0)
                sine, cosine = quarter_sincos(
                    jnp.full((SUB, LANES), cut_angle_ref[k], jnp.float32) * to_quarter
                )
                kept_all = jnp.full((SUB, LANES), path_ref[k], jnp.int32) == 0
                cut_size = cut_size * jnp.where(kept_all, cosine, sine)
            folded = tile_index & cut_mask
            for shift in (16, 8, 4, 2, 1):
                folded = folded ^ (folded >> shift)
            turns[0] = turns[0] + cut_turns + ((folded & 1) * 2).astype(jnp.float32)
            for k, place in enumerate(places):
                turns[1 + k] = turns[1 + k] + jnp.where((cut_mask & (1 << place)) != 0, 2.0, 0.0)
        sine, cosine = quarter_sincos(jnp.stack(turns))
        waves = [(cosine[k], sine[k]) for k in range(len(turns))]
        base, steps, row_waves = waves[0], waves[1 : 1 + len(places)], waves[1 + len(places) :]
        if layer == 0:
            base = (base[0] * cut_size, base[1] * cut_size)
        for tile in range(row_tiles):
            for part in range(2):
                r_tab[layer, part, tile * SUB : (tile + 1) * SUB] = row_waves[tile][part]
        x_waves = [base]
        for step in steps[:3]:
            x_waves = x_waves + [times(wave, step) for wave in x_waves]
        y_waves = [None]
        for step in steps[3:]:
            y_waves = y_waves + [
                step if wave is None else times(wave, step) for wave in y_waves
            ]
        y_waves[0] = (jnp.ones((SUB, LANES), jnp.float32), jnp.zeros((SUB, LANES), jnp.float32))
        for tab, values in ((x_tab, x_waves), (y_tab, y_waves)):
            for k, wave in enumerate(values):
                for part in range(2):
                    tab[layer, k, part] = wave[part]
        per_chunk = n // SUB

        def entry(y, x):
            row = pl.ds(y * SUB + x, 1)
            row_wave = tuple(
                jnp.broadcast_to(r_tab[layer, part, row, :], (SUB, LANES)) for part in range(2)
            )
            x_wave = (x_tab[layer, x, 0], x_tab[layer, x, 1])
            y_wave = (y_tab[layer, y, 0], y_tab[layer, y, 1])
            return times(times(x_wave, y_wave), row_wave)

        if far:
            for tile in range(half // SUB):
                for x in range(SUB):
                    at = pl.ds(pl.multiple_of((tile * SUB + x) * SUB, SUB), SUB)
                    y = last * per_chunk + top * (half // SUB) + tile
                    cosine, sine = entry(y, x)
                    cos_far[layer, at] = cosine
                    sin_far[layer, at] = sine
            return

        @pl.loop(0, row_tiles)
        def _(y):
            chunk = y // per_chunk
            start = lax.rem(y, per_chunk) * (SUB * SUB)
            for x in range(SUB):
                at = pl.ds(pl.multiple_of(start + x * SUB, SUB), SUB)
                cosine, sine = entry(y, x)
                cos_all[layer, chunk, at] = cosine
                sin_all[layer, chunk, at] = sine

    def layer_step(state, layer, outer, inner, cosine, sine):
        count = outer * inner

        def pieces(value):
            shaped = value.reshape(outer, 2, inner, LANES)
            return [shaped[:, t].reshape(count, LANES) for t in range(2)]

        def whole(parts):
            shaped = [part.reshape(outer, inner, LANES) for part in parts]
            return jnp.stack(shaped, axis=1).reshape(2 * count, LANES)

        real, imag = pieces(state[0]), pieces(state[1])
        joined = jnp.concatenate((real[0], imag[0], real[1], imag[1]), axis=1)
        high = joined.astype(jnp.bfloat16)
        rest = (joined - high.astype(jnp.float32)).astype(jnp.bfloat16)
        both = jnp.dot(
            jnp.concatenate((high, rest), axis=0),
            weights[layer],
            preferred_element_type=jnp.float32,
        )
        product = both[:count] + both[count:]
        columns = [product[:, k * LANES : (k + 1) * LANES] for k in range(4)]
        return times((whole(columns[0::2]), whole(columns[1::2])), (cosine, sine))

    def half_layers(reads, tables):
        states = [tuple(read(c) for c in range(2)) for read in reads]
        for layer in range(g - 1):
            for k, table in enumerate(tables):
                cosine, sine = table(layer)
                outer = states[k][0].shape[0] // (2 ** (layer + 1) * SUB)
                states[k] = layer_step(states[k], layer, outer, 2**layer * SUB, cosine, sine)
        return states

    def first_layers(jobs):
        def mine(side):
            return pl.ds(pl.multiple_of(side * half_rows, half_rows), half_rows)

        def read(chunk, side, c):
            start = pl.multiple_of(side * half * piece, half * piece)
            return recv[chunk, pl.ds(start + c, half_rows, stride=2), :]

        def table(chunk, side, layer):
            return cos_all[layer, chunk, mine(side)], sin_all[layer, chunk, mine(side)]

        states = half_layers(
            [functools.partial(read, *job) for job in jobs],
            [functools.partial(table, *job) for job in jobs],
        )
        for state, (chunk, side) in zip(states, jobs):
            for c in range(2):
                mixed[chunk, c, mine(side)] = state[c]

    def relay_layers():
        states = half_layers(
            [lambda c: relay_in[pl.ds(c, half_rows, stride=2), :]],
            [lambda layer: (cos_far[layer], sin_far[layer])],
        )
        for c in range(2):
            relay_out[c] = states[0][c]

    def last_layers(batches):
        def whole_step(batch, state, layer, outer, inner):
            cosine, sine = (
                jnp.concatenate([table[layer, chunk] for chunk in batch], axis=0)
                for table in (cos_all, sin_all)
            )
            return layer_step(state, layer, len(batch) * outer, inner, cosine, sine)

        states = []
        for batch in batches:
            state = tuple(
                jnp.concatenate([mixed[chunk, c] for chunk in batch], axis=0) for c in range(2)
            )
            state = whole_step(batch, state, g - 1, 1, half * SUB)
            for c in range(2):
                for k, chunk in enumerate(batch):
                    turned[chunk, c] = state[c][k * rows : (k + 1) * rows]
            states.append(
                tuple(
                    jnp.concatenate(
                        [
                            turned[chunk, c, pl.ds(low, n, stride=SUB), :]
                            for chunk in batch
                            for low in range(SUB)
                        ],
                        axis=0,
                    )
                    for c in range(2)
                )
            )
        for layer in range(g, layers):
            k = layer - g
            for b, batch in enumerate(batches):
                states[b] = whole_step(batch, states[b], layer, 2 ** (2 - k), 2**k * n)
        for state, batch in zip(states, batches):
            for k, chunk in enumerate(batch):
                base = spread(chunk, [(k, chunk_row(k)) for k in range(block_bits - 3)])
                for low in range(SUB):
                    start = pl.multiple_of(2 * (base + (low << block_bits)), 2 * n)
                    for c in range(2):
                        out_ref[pl.ds(start + c, n, stride=2), :] = state[c][
                            k * rows + low * n : k * rows + (low + 1) * n
                        ]

    @pl.when(top == 0)
    def _():
        pl.semaphore_wait(barrier, half - 1)
        send_relays()

    for small_copy in small_copies:
        small_copy.wait()
    make_table(0, mirror, far=True)

    @pl.when(top == 0)
    def _():
        for level in range(2):
            pl.semaphore_wait(came_sem.at[level], 2)
            send_column(0, level, 0)
        for off in range(1, columns):
            signal(seen_sem, me - column * 2 + lax.rem(column + off, columns) * 2)
        pl.semaphore_wait(seen_sem, columns - 1)

        @pl.when(spot >= quarter)
        def _():
            signal(go_sem, me + half)
            signal(go_sem, me + half - quarter)

        for level in range(2):
            for off in range(1, columns):
                send_column(0, level, off)
        send_near(0, chunks)
        send_columns(1, list(range(columns)))

    for layer in range(1, g - 1):
        make_table(layer, mirror, far=True)
    gate_copy.wait()

    @pl.loop(0, layers)
    def _(layer):
        make_weights(layer)

    for layer in range(1):
        make_table(layer, me)

    @pl.when(top == 1)
    def _():
        pl.semaphore_wait(go_sem, 1)
        send_relays()
        send_levels(0, list(range(1, columns)))
        send_near(0, early)

    for layer in range(1, layers):
        make_table(layer, me)

    pltpu.make_async_copy(relay_in, relay_in, relay_sem.at[0]).wait()
    relay_layers()
    for c in range(2):
        relay_result(c).start()

    @pl.when(top == 1)
    def _():
        send_near(early, chunks)

    for chunk in range(early):
        arrived(chunk, top)
    first_layers([(chunk, top) for chunk in range(early)])
    for chunk in range(early):
        arrived(chunk, 1 - top)
    first_layers([(chunk, 1 - top) for chunk in range(early)])
    last_layers([[chunk] for chunk in range(early)])

    for chunk in late:
        arrived(chunk, top)
    for chunk in late[:-1]:
        arrived(chunk, 1 - top)
    first_layers([(chunk, top) for chunk in late] + [(chunk, 1 - top) for chunk in late[:-1]])
    came = recv.at[0, pl.ds(0, 2 * half_rows)]
    pltpu.make_async_copy(came, came, relay_sem.at[2]).wait()
    last_layers([[chunk] for chunk in late])

    def wait_sent(semaphore, count):
        gone = amp_ref.at[pl.ds(0, count)]
        pltpu.make_async_remote_copy(
            src_ref=gone,
            dst_ref=recv.at[0, pl.ds(0, count)],
            send_sem=semaphore,
            recv_sem=recv_sem.at[0, 0],
            device_id={"hi": lax.rem(me + 1, n)},
            device_id_type=MESH,
        ).wait_send()

    for chunk in range(last):
        wait_sent(send_sem.at[chunk], (n - 1) * piece)
    wait_sent(send_sem.at[last], (n - 2) * piece)
    wait_sent(relay_sem.at[1], 2 * half_rows)


def one_exchange(
    amplitudes, gate_matrices, phase_qubits, phase_angles, cut_qubits, cut_angle, path_index
):
    g = lax.axis_size("hi").bit_length() - 1
    amp_count = amplitudes.shape[1]
    local_bits = amp_count.bit_length() - 1
    layers, pairs = phase_angles.shape
    cuts = cut_angle.shape[0]
    n = 2**g
    chunks = 2 ** (local_bits - g - 10)
    rows = n * SUB
    all_rows = amp_count // LANES
    row_tiles = n * chunks // SUB
    whole = amplitudes.reshape(2, all_rows, LANES).transpose(1, 0, 2).reshape(2 * all_rows, LANES)
    hbm = pl.BlockSpec(memory_space=pltpu.HBM)
    result = pl.pallas_call(
        functools.partial(circuit_kernel, g, local_bits, layers, pairs, cuts),
        out_shape=pltpu.VMEM((2 * all_rows, LANES), jnp.float32),
        in_specs=[hbm] * 7,
        out_specs=pl.BlockSpec(memory_space=pltpu.VMEM),
        scratch_shapes=[
            pltpu.SMEM((layers, 2, pairs), jnp.int32),
            pltpu.SMEM(phase_angles.shape, jnp.float32),
            pltpu.SMEM((2, cuts), jnp.int32),
            pltpu.SMEM(cut_angle.shape, jnp.float32),
            pltpu.SMEM(path_index.shape, jnp.int32),
            pltpu.VMEM((chunks, 2 * rows, LANES), jnp.float32),
            pltpu.VMEM((layers, 512, 512), jnp.bfloat16),
            pltpu.VMEM(gate_matrices.shape, jnp.bfloat16),
            pltpu.VMEM((layers, chunks, rows, LANES), jnp.float32),
            pltpu.VMEM((layers, chunks, rows, LANES), jnp.float32),
            pltpu.VMEM((layers, SUB, 2, SUB, LANES), jnp.float32),
            pltpu.VMEM((layers, row_tiles, 2, SUB, LANES), jnp.float32),
            pltpu.VMEM((layers, 2, row_tiles * SUB, LANES), jnp.float32),
            pltpu.VMEM((chunks, 2, rows, LANES), jnp.float32),
            pltpu.VMEM((chunks, 2, rows, LANES), jnp.float32),
            pltpu.VMEM((rows, LANES), jnp.float32),
            pltpu.VMEM((2, rows // 2, LANES), jnp.float32),
            pltpu.VMEM((g - 1, rows // 2, LANES), jnp.float32),
            pltpu.VMEM((g - 1, rows // 2, LANES), jnp.float32),
            pltpu.SemaphoreType.DMA((chunks,)),
            pltpu.SemaphoreType.DMA((chunks, 2)),
            pltpu.SemaphoreType.DMA((3,)),
            pltpu.SemaphoreType.DMA,
            pltpu.SemaphoreType.DMA((5,)),
            pltpu.SemaphoreType.REGULAR((2,)),
            pltpu.SemaphoreType.REGULAR,
            pltpu.SemaphoreType.REGULAR,
        ],
        compiler_params=pltpu.CompilerParams(collective_id=0, has_side_effects=True),
    )(
        whole, gate_matrices, phase_qubits.transpose(0, 2, 1), phase_angles,
        cut_qubits.transpose(1, 0), cut_angle, path_index,
    )
    return result.reshape(all_rows, 2, LANES).transpose(1, 0, 2).reshape(2, amp_count)


def from_partner(value, axis, bit):
    return lax.ppermute(value, axis, [(i, i ^ 1 << bit) for i in range(lax.axis_size(axis))])


def real_form(matrix):
    real_part = matrix[0].astype(jnp.float32)
    imag_part = matrix[1].astype(jnp.float32)
    upper_rows = jnp.stack((real_part, -imag_part), axis=1)
    lower_rows = jnp.stack((imag_part, real_part), axis=1)
    stacked = jnp.stack((upper_rows, lower_rows), axis=0)
    return stacked.reshape(2, 2, 64, 2, 2, 64)


def apply_gate(amps_now, matrix, target, local_bits):
    shaped = amps_now.reshape(2, 2 ** (local_bits - 1 - target), 2, 2 ** (target - 7), 2, 64)
    result = jnp.einsum(
        "wxyzbd,zabced->waxcey", real_form(matrix), shaped, precision=lax.Precision.HIGHEST
    )
    return result.reshape(2, -1)


def rotate(amps_now, theta):
    cosine = jnp.cos(theta)
    sine = jnp.sin(theta)
    return jnp.stack(
        (cosine * amps_now[0] - sine * amps_now[1], sine * amps_now[0] + cosine * amps_now[1])
    )


def bit_of(index_all, qubit):
    return jnp.bitwise_and(jnp.right_shift(index_all, qubit), 1)


def located(qubit, first_open, global_count, local_bits):
    moved_up = (qubit >= 7 + first_open) & (qubit < 7 + global_count)
    moved_down = (qubit >= local_bits + first_open) & (qubit < local_bits + global_count)
    return jnp.where(
        moved_up, qubit - 7 + local_bits, jnp.where(moved_down, qubit - local_bits + 7, qubit)
    )


def enter_qubit(amps_now, bit_number, local_bits, device_place):
    shaped = amps_now.reshape(2, 2 ** (local_bits - 8 - bit_number), 2, 2**bit_number, 128)
    zero_half = shaped[:, :, 0]
    one_half = shaped[:, :, 1]
    upper_side = jnp.bitwise_and(jnp.right_shift(device_place, bit_number), 1) == 1
    kept_half = jnp.where(upper_side, one_half, zero_half)
    sent_half = jnp.where(upper_side, zero_half, one_half)
    came_half = from_partner(sent_half, "hi", bit_number)
    new_zero = jnp.where(upper_side, came_half, kept_half)
    new_one = jnp.where(upper_side, kept_half, came_half)
    return jnp.stack((new_zero, new_one), axis=2).reshape(2, -1)


def shards(
    amplitudes, gate_matrices, phase_qubits, phase_angles, cut_qubits, cut_angle, path_index
):
    global_count = lax.axis_size("hi").bit_length() - 1
    amp_count = amplitudes.shape[1]
    local_bits = amp_count.bit_length() - 1
    device_place = lax.axis_index("hi")
    index_all = device_place * amp_count + lax.iota(jnp.int32, amp_count)
    layer_count = gate_matrices.shape[0]
    result = amplitudes
    for layer_number in range(layer_count):
        if layer_number < global_count:
            result = enter_qubit(result, layer_number, local_bits, device_place)
            target = 7 + layer_number
        else:
            if layer_number == global_count:
                shaped = result.reshape(2, 2**global_count, 2 ** (local_bits - global_count))
                result = lax.all_to_all(
                    shaped, "hi", split_axis=1, concat_axis=1, tiled=True
                ).reshape(2, -1)
            target = local_bits - 2 * global_count + layer_number
        result = apply_gate(result, gate_matrices[layer_number], target, local_bits)
        theta = jnp.zeros((amp_count,), jnp.float32)
        for pair_number in range(phase_qubits.shape[1]):
            first_pos = located(
                phase_qubits[layer_number, pair_number, 0], global_count, global_count, local_bits
            )
            second_pos = located(
                phase_qubits[layer_number, pair_number, 1], global_count, global_count, local_bits
            )
            both_bits = bit_of(index_all, first_pos) * bit_of(index_all, second_pos)
            theta = theta + phase_angles[layer_number, pair_number] * both_bits.astype(jnp.float32)
        result = rotate(result, theta)
        if layer_number == 0:
            for cut_number in range(cut_qubits.shape[0]):
                first_cut = located(
                    cut_qubits[cut_number, 0], global_count, global_count, local_bits
                )
                second_cut = located(
                    cut_qubits[cut_number, 1], global_count, global_count, local_bits
                )
                parity = jnp.bitwise_xor(
                    bit_of(index_all, first_cut), bit_of(index_all, second_cut)
                )
                signs = (1 - 2 * parity).astype(jnp.float32)
                chosen = path_index[cut_number] == 0
                angle_now = cut_angle[cut_number]
                keep_part = jnp.where(chosen, jnp.cos(angle_now), jnp.zeros_like(angle_now))
                turn_part = jnp.where(chosen, jnp.zeros_like(angle_now), jnp.sin(angle_now))
                result = jnp.stack(
                    (
                        keep_part * result[0] + turn_part * signs * result[1],
                        keep_part * result[1] - turn_part * signs * result[0],
                    )
                )
    return result


def any_slice(amplitudes, gate_matrices, *rest):
    g = lax.axis_size("hi").bit_length() - 1
    local_bits = amplitudes.shape[1].bit_length() - 1
    late_layers = gate_matrices.shape[0] - g
    fits = 4 <= g <= local_bits - g - 7 and local_bits - g >= 12 and 0 < late_layers <= 3
    plan = one_exchange if fits else shards
    return plan(amplitudes, gate_matrices, *rest)


def solution(mesh):
    placed = (
        P(None, ("paths", "hi")),
        P(),
        P("paths", None, None),
        P("paths", None),
        P("paths", None),
        P("paths"),
        P("paths"),
    )
    return jax.shard_map(
        any_slice, mesh=mesh, in_specs=placed, out_specs=P(None, ("paths", "hi")), check_vma=False
    )
```

```python
import functools
import math

import jax
import jax.numpy as jnp
from jax import lax
from jax.experimental import pallas as pl
from jax.experimental.pallas import tpu as pltpu
from jax.sharding import PartitionSpec as P

LANES = 128
SUB = 8
MESH = pl.DeviceIdType.MESH


def quarter_sincos(turns):
    whole = jnp.floor(turns + 0.5)
    rest = turns - whole
    square = rest * rest
    half_pi = math.pi / 2
    sin_terms = [(-1) ** k * half_pi ** (2 * k + 1) / math.factorial(2 * k + 1) for k in range(5)]
    cos_terms = [(-1) ** k * half_pi ** (2 * k) / math.factorial(2 * k) for k in range(6)]
    sine = jnp.full_like(square, sin_terms[-1])
    for term in sin_terms[-2::-1]:
        sine = sine * square + term
    sine = sine * rest
    cosine = jnp.full_like(square, cos_terms[-1])
    for term in cos_terms[-2::-1]:
        cosine = cosine * square + term
    count = whole.astype(jnp.int32)
    odd = (count & 1) == 1
    sin_out = jnp.where(odd, cosine, sine)
    cos_out = jnp.where(odd, sine, cosine)
    sin_out = jnp.where((count & 2) == 2, -sin_out, sin_out)
    cos_out = jnp.where(((count + 1) & 2) == 2, -cos_out, cos_out)
    return sin_out, cos_out


def swap_half(value):
    return pltpu.roll(value, LANES // 2, axis=1)


def spread(value, moves):
    total = None
    for a, b in moves:
        term = ((value >> a) & 1) << b
        total = term if total is None else total + term
    return total


def times(a, b):
    return a[0] * b[0] - a[1] * b[1], a[0] * b[1] + a[1] * b[0]


def circuit_kernel(
    g, local_bits, layers, pairs, cuts,
    amp_ref, gate_ref, qubit_in, angle_in, cut_qubit_in, cut_angle_in, path_in, out_ref,
    qubit_ref, angle_ref, cut_qubit_ref, cut_angle_ref, path_ref,
    recv, weights, gates, cos_all, sin_all, x_tab, y_tab, r_tab, mixed, turned,
    relay_in, relay_out, cos_far, sin_far,
    send_sem, recv_sem, relay_sem, gate_sem, small_sem, came_sem, seen_sem, go_sem,
):
    n = 2**g
    half, quarter = n // 2, n // 4
    block_bits = local_bits - g - 7
    chunks = 2 ** (block_bits - 3)
    piece = 2 * SUB
    rows = n * SUB
    half_rows = half * SUB
    early = chunks // 2
    late = list(range(early, chunks))
    last = chunks - 1
    me = lax.axis_index("hi")
    top = me // half
    spot = lax.rem(me, half)
    columns = quarter // 2
    column = lax.rem(spot // 2, columns)
    mirror = (1 - top) * half + lax.rem(spot + top * quarter, half)

    def block_rows(owner, chunk):
        return pl.ds(pl.multiple_of((owner * chunks + chunk) * piece, piece), piece)

    def slot_rows(source):
        return pl.ds(pl.multiple_of(source * piece, piece), piece)

    def half_slots(side):
        return pl.ds(pl.multiple_of(side * half * piece, half * piece), half * piece)

    def send(chunk, peer):
        pltpu.make_async_remote_copy(
            src_ref=amp_ref.at[block_rows(peer, chunk)],
            dst_ref=recv.at[chunk, slot_rows(me)],
            send_sem=send_sem.at[chunk],
            recv_sem=recv_sem.at[chunk, top],
            device_id={"hi": peer},
            device_id_type=MESH,
        ).start()

    def arrived(chunk, side):
        here = recv.at[chunk, half_slots(side)]
        pltpu.make_async_copy(here, here, recv_sem.at[chunk, side]).wait()

    def relay_piece(off):
        target = relay_in.at[pl.ds(pl.multiple_of(spot * piece, piece), piece)]
        if off == 0:
            return pltpu.make_async_copy(
                amp_ref.at[block_rows(mirror, last)], target, relay_sem.at[0]
            )
        peer = lax.rem(spot + off, half)
        return pltpu.make_async_remote_copy(
            src_ref=amp_ref.at[
                block_rows((1 - top) * half + lax.rem(peer + top * quarter, half), last)
            ],
            dst_ref=target,
            send_sem=send_sem.at[last],
            recv_sem=relay_sem.at[0],
            device_id={"hi": top * half + peer},
            device_id_type=MESH,
        )

    def send_relays():
        for off in range(half):
            relay_piece(off).start()

    def relay_result(c):
        mine = pl.ds(pl.multiple_of(top * half_rows, half_rows), half_rows)
        return pltpu.make_async_remote_copy(
            src_ref=relay_out.at[c],
            dst_ref=mixed.at[last, c, mine],
            send_sem=relay_sem.at[1],
            recv_sem=relay_sem.at[2],
            device_id={"hi": mirror},
            device_id_type=MESH,
        )

    def signal(semaphore, peer):
        pl.semaphore_signal(semaphore, inc=1, device_id={"hi": peer}, device_id_type=MESH)

    barrier = pltpu.get_barrier_semaphore()

    @pl.when(top == 0)
    def _():
        for level in range(2):
            for core in range(2):
                signal(barrier, half + level * quarter + column * 2 + core)
        for off in range(1, half):
            signal(barrier, lax.rem(spot + off, half))

    smalls = (
        (qubit_in, qubit_ref),
        (angle_in, angle_ref),
        (cut_qubit_in, cut_qubit_ref),
        (cut_angle_in, cut_angle_ref),
        (path_in, path_ref),
    )
    small_copies = [
        pltpu.make_async_copy(source, target, small_sem.at[k])
        for k, (source, target) in enumerate(smalls)
    ]
    for small_copy in small_copies:
        small_copy.start()
    gate_copy = pltpu.make_async_copy(gate_ref, gates, gate_sem)
    gate_copy.start()

    @pl.loop(0, chunks)
    def _(chunk):
        pltpu.make_async_copy(
            amp_ref.at[block_rows(me, chunk)],
            recv.at[chunk, slot_rows(me)],
            recv_sem.at[chunk, top],
        ).start()

    def send_near(first, last):
        @pl.loop(first, last)
        def _(chunk):
            for off in range(1, half):
                send(chunk, top * half + lax.rem(spot + off, half))

    def send_column(chunk, level, off):
        there = (1 - top) * half + level * quarter + lax.rem(column + off, columns) * 2
        for core in range(2):
            send(chunk, there + lax.rem(spot + core, 2))

    def send_columns(first, offs):
        @pl.loop(first, last)
        def _(chunk):
            for level in range(2):
                for off in offs:
                    send_column(chunk, level, off)

    def send_levels(first, offs):
        for level in range(2):
            @pl.loop(first, last)
            def _(chunk):
                for off in offs:
                    send_column(chunk, level, off)

    @pl.when(top == 1)
    def _():
        pl.semaphore_wait(barrier, 4)
        for level in range(2):
            for core in range(2):
                signal(came_sem.at[spot // quarter], level * quarter + column * 2 + core)
        send_columns(0, [0])

    low_lanes = lax.broadcasted_iota(jnp.int32, (64, LANES), 1) < 64
    blank = jnp.zeros((64, LANES), jnp.float32)

    def make_weights(layer):
        flat = [gates[layer, part].astype(jnp.float32).T for part in range(2)]
        for t in range(2):
            plain = [part[t * 64 : (t + 1) * 64] for part in flat]
            turned_part = [swap_half(part) for part in plain]
            for c in range(2):
                for t_out in range(2):
                    for c_out in range(2):
                        low_from, high_from = (
                            (plain, turned_part) if t_out == 0 else (turned_part, plain)
                        )
                        part = c ^ c_out
                        upper = jnp.where(low_lanes, low_from[part], blank)
                        lower = jnp.where(low_lanes, blank, high_from[part])
                        if c == 1 and c_out == 0:
                            upper, lower = -upper, -lower
                        block = jnp.concatenate((upper, lower), axis=0).astype(jnp.bfloat16)
                        row, column = (2 * t + c) * LANES, (2 * t_out + c_out) * LANES
                        weights[layer, row : row + LANES, column : column + LANES] = block

    def chunk_row(k):
        return block_bits + 3 + k if 10 + k < 7 + g else 3 + k

    lane = lax.broadcasted_iota(jnp.int32, (SUB, LANES), 1)
    sub = lax.broadcasted_iota(jnp.int32, (SUB, LANES), 0)
    to_quarter = 2.0 / math.pi
    chunk_places = [10 + k for k in range(block_bits - 3)]

    def entered(layer, q):
        if layer < g:
            up = (q >= 7) & (q <= 7 + layer)
            down = (q >= local_bits) & (q <= local_bits + layer)
            moved = local_bits - 7
            return q + jnp.where(up, moved, 0) - jnp.where(down, moved, 0)
        shift = jnp.where(q >= 7, local_bits - 7, 0)
        shift = jnp.where(q >= 7 + g, 0, shift)
        shift = jnp.where(q >= local_bits - g, 7 + g - local_bits, shift)
        shift = jnp.where(q >= local_bits, -g, shift)
        return q + shift

    def make_table(layer, owner, far=False):
        if layer < g:
            tile_places = [7, 8, 9]
            row_places = [local_bits + k for k in range(g)]
        else:
            tile_places = [local_bits + k for k in range(3)]
            row_places = [local_bits + k for k in range(3, g)] + [7, 8, 9]
        places = row_places + chunk_places
        masks, angles = [], []
        for k in range(pairs):
            masks.append(
                (jnp.int32(1) << entered(layer, qubit_ref[layer, 0, k]))
                | (jnp.int32(1) << entered(layer, qubit_ref[layer, 1, k]))
            )
            angles.append(angle_ref[layer, k] * to_quarter)

        def total(index, pick):
            turns = jnp.zeros((SUB, LANES), jnp.float32)
            for k in range(pairs):
                mask, angle = pick(masks[k], angles[k])
                turns = turns + jnp.where((index & mask) == mask, angle, 0.0)
            return turns

        tile_index = (
            lane
            + spread(sub, list(enumerate(tile_places)))
            + spread(owner, [(k, local_bits - g + k) for k in range(g)])
        )
        turns = [total(tile_index, lambda mask, angle: (mask, angle))]
        for place in places:
            bit = 1 << place
            turns.append(
                total(
                    tile_index | bit,
                    lambda mask, angle: (
                        mask, jnp.where(((mask & bit) != 0) & (mask != bit), angle, 0.0)
                    ),
                )
            )
        row_tiles = 2 ** len(places) // SUB
        for tile in range(row_tiles):
            row_index = spread(sub, list(enumerate(places[:3]))) + sum(
                (1 << place) if (tile >> k) & 1 else 0 for k, place in enumerate(places[3:])
            )
            turns.append(total(row_index, lambda mask, angle: (mask, angle)))
        if layer == 0:
            cut_mask = jnp.int32(0)
            cut_turns = jnp.float32(0)
            cut_size = jnp.full((SUB, LANES), 1.0, jnp.float32)
            for k in range(cuts):
                kept = path_ref[k] == 0
                bits = (jnp.int32(1) << entered(0, cut_qubit_ref[0, k])) ^ (
                    jnp.int32(1) << entered(0, cut_qubit_ref[1, k])
                )
                cut_mask = cut_mask ^ jnp.where(kept, 0, bits)
                cut_turns = cut_turns - jnp.where(kept, 0.0, 1.0)
                sine, cosine = quarter_sincos(
                    jnp.full((SUB, LANES), cut_angle_ref[k], jnp.float32) * to_quarter
                )
                kept_all = jnp.full((SUB, LANES), path_ref[k], jnp.int32) == 0
                cut_size = cut_size * jnp.where(kept_all, cosine, sine)
            folded = tile_index & cut_mask
            for shift in (16, 8, 4, 2, 1):
                folded = folded ^ (folded >> shift)
            turns[0] = turns[0] + cut_turns + ((folded & 1) * 2).astype(jnp.float32)
            for k, place in enumerate(places):
                turns[1 + k] = turns[1 + k] + jnp.where((cut_mask & (1 << place)) != 0, 2.0, 0.0)
        sine, cosine = quarter_sincos(jnp.stack(turns))
        waves = [(cosine[k], sine[k]) for k in range(len(turns))]
        base, steps, row_waves = waves[0], waves[1 : 1 + len(places)], waves[1 + len(places) :]
        if layer == 0:
            base = (base[0] * cut_size, base[1] * cut_size)
        for tile in range(row_tiles):
            for part in range(2):
                r_tab[layer, part, tile * SUB : (tile + 1) * SUB] = row_waves[tile][part]
        x_waves = [base]
        for step in steps[:3]:
            x_waves = x_waves + [times(wave, step) for wave in x_waves]
        y_waves = [None]
        for step in steps[3:]:
            y_waves = y_waves + [
                step if wave is None else times(wave, step) for wave in y_waves
            ]
        y_waves[0] = (jnp.ones((SUB, LANES), jnp.float32), jnp.zeros((SUB, LANES), jnp.float32))
        for tab, values in ((x_tab, x_waves), (y_tab, y_waves)):
            for k, wave in enumerate(values):
                for part in range(2):
                    tab[layer, k, part] = wave[part]
        per_chunk = n // SUB

        def entry(y, x):
            row = pl.ds(y * SUB + x, 1)
            row_wave = tuple(
                jnp.broadcast_to(r_tab[layer, part, row, :], (SUB, LANES)) for part in range(2)
            )
            x_wave = (x_tab[layer, x, 0], x_tab[layer, x, 1])
            y_wave = (y_tab[layer, y, 0], y_tab[layer, y, 1])
            return times(times(x_wave, y_wave), row_wave)

        if far:
            for tile in range(half // SUB):
                for x in range(SUB):
                    at = pl.ds(pl.multiple_of((tile * SUB + x) * SUB, SUB), SUB)
                    y = last * per_chunk + top * (half // SUB) + tile
                    cosine, sine = entry(y, x)
                    cos_far[layer, at] = cosine
                    sin_far[layer, at] = sine
            return

        @pl.loop(0, row_tiles)
        def _(y):
            chunk = y // per_chunk
            start = lax.rem(y, per_chunk) * (SUB * SUB)
            for x in range(SUB):
                at = pl.ds(pl.multiple_of(start + x * SUB, SUB), SUB)
                cosine, sine = entry(y, x)
                cos_all[layer, chunk, at] = cosine
                sin_all[layer, chunk, at] = sine

    def layer_step(state, layer, outer, inner, cosine, sine):
        count = outer * inner

        def pieces(value):
            shaped = value.reshape(outer, 2, inner, LANES)
            return [shaped[:, t].reshape(count, LANES) for t in range(2)]

        def whole(parts):
            shaped = [part.reshape(outer, inner, LANES) for part in parts]
            return jnp.stack(shaped, axis=1).reshape(2 * count, LANES)

        real, imag = pieces(state[0]), pieces(state[1])
        joined = jnp.concatenate((real[0], imag[0], real[1], imag[1]), axis=1)
        high = joined.astype(jnp.bfloat16)
        rest = (joined - high.astype(jnp.float32)).astype(jnp.bfloat16)
        both = jnp.dot(
            jnp.concatenate((high, rest), axis=0),
            weights[layer],
            preferred_element_type=jnp.float32,
        )
        product = both[:count] + both[count:]
        columns = [product[:, k * LANES : (k + 1) * LANES] for k in range(4)]
        return times((whole(columns[0::2]), whole(columns[1::2])), (cosine, sine))

    def half_layers(reads, tables):
        states = [tuple(read(c) for c in range(2)) for read in reads]
        for layer in range(g - 1):
            for k, table in enumerate(tables):
                cosine, sine = table(layer)
                outer = states[k][0].shape[0] // (2 ** (layer + 1) * SUB)
                states[k] = layer_step(states[k], layer, outer, 2**layer * SUB, cosine, sine)
        return states

    def first_layers(jobs):
        def mine(side):
            return pl.ds(pl.multiple_of(side * half_rows, half_rows), half_rows)

        def read(chunk, side, c):
            start = pl.multiple_of(side * half * piece, half * piece)
            return recv[chunk, pl.ds(start + c, half_rows, stride=2), :]

        def table(chunk, side, layer):
            return cos_all[layer, chunk, mine(side)], sin_all[layer, chunk, mine(side)]

        states = half_layers(
            [functools.partial(read, *job) for job in jobs],
            [functools.partial(table, *job) for job in jobs],
        )
        for state, (chunk, side) in zip(states, jobs):
            for c in range(2):
                mixed[chunk, c, mine(side)] = state[c]

    def relay_layers():
        states = half_layers(
            [lambda c: relay_in[pl.ds(c, half_rows, stride=2), :]],
            [lambda layer: (cos_far[layer], sin_far[layer])],
        )
        for c in range(2):
            relay_out[c] = states[0][c]

    def last_layers(batches):
        def whole_step(batch, state, layer, outer, inner):
            cosine, sine = (
                jnp.concatenate([table[layer, chunk] for chunk in batch], axis=0)
                for table in (cos_all, sin_all)
            )
            return layer_step(state, layer, len(batch) * outer, inner, cosine, sine)

        states = []
        for batch in batches:
            state = tuple(
                jnp.concatenate([mixed[chunk, c] for chunk in batch], axis=0) for c in range(2)
            )
            state = whole_step(batch, state, g - 1, 1, half * SUB)
            for c in range(2):
                for k, chunk in enumerate(batch):
                    turned[chunk, c] = state[c][k * rows : (k + 1) * rows]
            states.append(
                tuple(
                    jnp.concatenate(
                        [
                            turned[chunk, c, pl.ds(low, n, stride=SUB), :]
                            for chunk in batch
                            for low in range(SUB)
                        ],
                        axis=0,
                    )
                    for c in range(2)
                )
            )
        for layer in range(g, layers):
            k = layer - g
            for b, batch in enumerate(batches):
                states[b] = whole_step(batch, states[b], layer, 2 ** (2 - k), 2**k * n)
        for state, batch in zip(states, batches):
            for k, chunk in enumerate(batch):
                base = spread(chunk, [(k, chunk_row(k)) for k in range(block_bits - 3)])
                for low in range(SUB):
                    start = pl.multiple_of(2 * (base + (low << block_bits)), 2 * n)
                    for c in range(2):
                        out_ref[pl.ds(start + c, n, stride=2), :] = state[c][
                            k * rows + low * n : k * rows + (low + 1) * n
                        ]

    @pl.when(top == 0)
    def _():
        pl.semaphore_wait(barrier, half - 1)
        send_relays()

    for small_copy in small_copies:
        small_copy.wait()
    make_table(0, mirror, far=True)

    @pl.when(top == 0)
    def _():
        for level in range(2):
            pl.semaphore_wait(came_sem.at[level], 2)
            send_column(0, level, 0)
        for off in range(1, columns):
            signal(seen_sem, me - column * 2 + lax.rem(column + off, columns) * 2)
        pl.semaphore_wait(seen_sem, columns - 1)

        @pl.when(spot >= quarter)
        def _():
            signal(go_sem, me + half)
            signal(go_sem, me + half - quarter)

        for level in range(2):
            for off in range(1, columns):
                send_column(0, level, off)
        send_near(0, early)
        send_columns(1, list(range(columns)))

    for layer in range(1, g - 1):
        make_table(layer, mirror, far=True)
    gate_copy.wait()

    @pl.loop(0, layers)
    def _(layer):
        make_weights(layer)

    for layer in range(1):
        make_table(layer, me)

    @pl.when(top == 1)
    def _():
        pl.semaphore_wait(go_sem, 1)
        send_relays()
        send_levels(0, list(range(1, columns)))
        send_near(0, early)

    for layer in range(1, layers):
        make_table(layer, me)

    pltpu.make_async_copy(relay_in, relay_in, relay_sem.at[0]).wait()
    relay_layers()
    for c in range(2):
        relay_result(c).start()

    send_near(early, chunks)

    for chunk in range(early):
        arrived(chunk, top)
    first_layers([(chunk, top) for chunk in range(early)])
    for chunk in range(early):
        arrived(chunk, 1 - top)
    first_layers([(chunk, 1 - top) for chunk in range(early)])
    last_layers([[chunk] for chunk in range(early)])

    for chunk in late:
        arrived(chunk, top)
    for chunk in late[:-1]:
        arrived(chunk, 1 - top)
    first_layers([(chunk, top) for chunk in late] + [(chunk, 1 - top) for chunk in late[:-1]])
    came = recv.at[0, pl.ds(0, 2 * half_rows)]
    pltpu.make_async_copy(came, came, relay_sem.at[2]).wait()
    last_layers([[chunk] for chunk in late])

    def wait_sent(semaphore, count):
        gone = amp_ref.at[pl.ds(0, count)]
        pltpu.make_async_remote_copy(
            src_ref=gone,
            dst_ref=recv.at[0, pl.ds(0, count)],
            send_sem=semaphore,
            recv_sem=recv_sem.at[0, 0],
            device_id={"hi": lax.rem(me + 1, n)},
            device_id_type=MESH,
        ).wait_send()

    for chunk in range(last):
        wait_sent(send_sem.at[chunk], (n - 1) * piece)
    wait_sent(send_sem.at[last], (n - 2) * piece)
    wait_sent(relay_sem.at[1], 2 * half_rows)


def one_exchange(
    amplitudes, gate_matrices, phase_qubits, phase_angles, cut_qubits, cut_angle, path_index
):
    g = lax.axis_size("hi").bit_length() - 1
    amp_count = amplitudes.shape[1]
    local_bits = amp_count.bit_length() - 1
    layers, pairs = phase_angles.shape
    cuts = cut_angle.shape[0]
    n = 2**g
    chunks = 2 ** (local_bits - g - 10)
    rows = n * SUB
    all_rows = amp_count // LANES
    row_tiles = n * chunks // SUB
    whole = amplitudes.reshape(2, all_rows, LANES).transpose(1, 0, 2).reshape(2 * all_rows, LANES)
    hbm = pl.BlockSpec(memory_space=pltpu.HBM)
    result = pl.pallas_call(
        functools.partial(circuit_kernel, g, local_bits, layers, pairs, cuts),
        out_shape=pltpu.VMEM((2 * all_rows, LANES), jnp.float32),
        in_specs=[hbm] * 7,
        out_specs=pl.BlockSpec(memory_space=pltpu.VMEM),
        scratch_shapes=[
            pltpu.SMEM((layers, 2, pairs), jnp.int32),
            pltpu.SMEM(phase_angles.shape, jnp.float32),
            pltpu.SMEM((2, cuts), jnp.int32),
            pltpu.SMEM(cut_angle.shape, jnp.float32),
            pltpu.SMEM(path_index.shape, jnp.int32),
            pltpu.VMEM((chunks, 2 * rows, LANES), jnp.float32),
            pltpu.VMEM((layers, 512, 512), jnp.bfloat16),
            pltpu.VMEM(gate_matrices.shape, jnp.bfloat16),
            pltpu.VMEM((layers, chunks, rows, LANES), jnp.float32),
            pltpu.VMEM((layers, chunks, rows, LANES), jnp.float32),
            pltpu.VMEM((layers, SUB, 2, SUB, LANES), jnp.float32),
            pltpu.VMEM((layers, row_tiles, 2, SUB, LANES), jnp.float32),
            pltpu.VMEM((layers, 2, row_tiles * SUB, LANES), jnp.float32),
            pltpu.VMEM((chunks, 2, rows, LANES), jnp.float32),
            pltpu.VMEM((chunks, 2, rows, LANES), jnp.float32),
            pltpu.VMEM((rows, LANES), jnp.float32),
            pltpu.VMEM((2, rows // 2, LANES), jnp.float32),
            pltpu.VMEM((g - 1, rows // 2, LANES), jnp.float32),
            pltpu.VMEM((g - 1, rows // 2, LANES), jnp.float32),
            pltpu.SemaphoreType.DMA((chunks,)),
            pltpu.SemaphoreType.DMA((chunks, 2)),
            pltpu.SemaphoreType.DMA((3,)),
            pltpu.SemaphoreType.DMA,
            pltpu.SemaphoreType.DMA((5,)),
            pltpu.SemaphoreType.REGULAR((2,)),
            pltpu.SemaphoreType.REGULAR,
            pltpu.SemaphoreType.REGULAR,
        ],
        compiler_params=pltpu.CompilerParams(collective_id=0, has_side_effects=True),
    )(
        whole, gate_matrices, phase_qubits.transpose(0, 2, 1), phase_angles,
        cut_qubits.transpose(1, 0), cut_angle, path_index,
    )
    return result.reshape(all_rows, 2, LANES).transpose(1, 0, 2).reshape(2, amp_count)


def from_partner(value, axis, bit):
    return lax.ppermute(value, axis, [(i, i ^ 1 << bit) for i in range(lax.axis_size(axis))])


def real_form(matrix):
    real_part = matrix[0].astype(jnp.float32)
    imag_part = matrix[1].astype(jnp.float32)
    upper_rows = jnp.stack((real_part, -imag_part), axis=1)
    lower_rows = jnp.stack((imag_part, real_part), axis=1)
    stacked = jnp.stack((upper_rows, lower_rows), axis=0)
    return stacked.reshape(2, 2, 64, 2, 2, 64)


def apply_gate(amps_now, matrix, target, local_bits):
    shaped = amps_now.reshape(2, 2 ** (local_bits - 1 - target), 2, 2 ** (target - 7), 2, 64)
    result = jnp.einsum(
        "wxyzbd,zabced->waxcey", real_form(matrix), shaped, precision=lax.Precision.HIGHEST
    )
    return result.reshape(2, -1)


def rotate(amps_now, theta):
    cosine = jnp.cos(theta)
    sine = jnp.sin(theta)
    return jnp.stack(
        (cosine * amps_now[0] - sine * amps_now[1], sine * amps_now[0] + cosine * amps_now[1])
    )


def bit_of(index_all, qubit):
    return jnp.bitwise_and(jnp.right_shift(index_all, qubit), 1)


def located(qubit, first_open, global_count, local_bits):
    moved_up = (qubit >= 7 + first_open) & (qubit < 7 + global_count)
    moved_down = (qubit >= local_bits + first_open) & (qubit < local_bits + global_count)
    return jnp.where(
        moved_up, qubit - 7 + local_bits, jnp.where(moved_down, qubit - local_bits + 7, qubit)
    )


def enter_qubit(amps_now, bit_number, local_bits, device_place):
    shaped = amps_now.reshape(2, 2 ** (local_bits - 8 - bit_number), 2, 2**bit_number, 128)
    zero_half = shaped[:, :, 0]
    one_half = shaped[:, :, 1]
    upper_side = jnp.bitwise_and(jnp.right_shift(device_place, bit_number), 1) == 1
    kept_half = jnp.where(upper_side, one_half, zero_half)
    sent_half = jnp.where(upper_side, zero_half, one_half)
    came_half = from_partner(sent_half, "hi", bit_number)
    new_zero = jnp.where(upper_side, came_half, kept_half)
    new_one = jnp.where(upper_side, kept_half, came_half)
    return jnp.stack((new_zero, new_one), axis=2).reshape(2, -1)


def shards(
    amplitudes, gate_matrices, phase_qubits, phase_angles, cut_qubits, cut_angle, path_index
):
    global_count = lax.axis_size("hi").bit_length() - 1
    amp_count = amplitudes.shape[1]
    local_bits = amp_count.bit_length() - 1
    device_place = lax.axis_index("hi")
    index_all = device_place * amp_count + lax.iota(jnp.int32, amp_count)
    layer_count = gate_matrices.shape[0]
    result = amplitudes
    for layer_number in range(layer_count):
        if layer_number < global_count:
            result = enter_qubit(result, layer_number, local_bits, device_place)
            target = 7 + layer_number
        else:
            if layer_number == global_count:
                shaped = result.reshape(2, 2**global_count, 2 ** (local_bits - global_count))
                result = lax.all_to_all(
                    shaped, "hi", split_axis=1, concat_axis=1, tiled=True
                ).reshape(2, -1)
            target = local_bits - 2 * global_count + layer_number
        result = apply_gate(result, gate_matrices[layer_number], target, local_bits)
        theta = jnp.zeros((amp_count,), jnp.float32)
        for pair_number in range(phase_qubits.shape[1]):
            first_pos = located(
                phase_qubits[layer_number, pair_number, 0], global_count, global_count, local_bits
            )
            second_pos = located(
                phase_qubits[layer_number, pair_number, 1], global_count, global_count, local_bits
            )
            both_bits = bit_of(index_all, first_pos) * bit_of(index_all, second_pos)
            theta = theta + phase_angles[layer_number, pair_number] * both_bits.astype(jnp.float32)
        result = rotate(result, theta)
        if layer_number == 0:
            for cut_number in range(cut_qubits.shape[0]):
                first_cut = located(
                    cut_qubits[cut_number, 0], global_count, global_count, local_bits
                )
                second_cut = located(
                    cut_qubits[cut_number, 1], global_count, global_count, local_bits
                )
                parity = jnp.bitwise_xor(
                    bit_of(index_all, first_cut), bit_of(index_all, second_cut)
                )
                signs = (1 - 2 * parity).astype(jnp.float32)
                chosen = path_index[cut_number] == 0
                angle_now = cut_angle[cut_number]
                keep_part = jnp.where(chosen, jnp.cos(angle_now), jnp.zeros_like(angle_now))
                turn_part = jnp.where(chosen, jnp.zeros_like(angle_now), jnp.sin(angle_now))
                result = jnp.stack(
                    (
                        keep_part * result[0] + turn_part * signs * result[1],
                        keep_part * result[1] - turn_part * signs * result[0],
                    )
                )
    return result


def any_slice(amplitudes, gate_matrices, *rest):
    g = lax.axis_size("hi").bit_length() - 1
    local_bits = amplitudes.shape[1].bit_length() - 1
    late_layers = gate_matrices.shape[0] - g
    fits = 4 <= g <= local_bits - g - 7 and local_bits - g >= 12 and 0 < late_layers <= 3
    plan = one_exchange if fits else shards
    return plan(amplitudes, gate_matrices, *rest)


def solution(mesh):
    placed = (
        P(None, ("paths", "hi")),
        P(),
        P("paths", None, None),
        P("paths", None),
        P("paths", None),
        P("paths"),
        P("paths"),
    )
    return jax.shard_map(
        any_slice, mesh=mesh, in_specs=placed, out_specs=P(None, ("paths", "hi")), check_vma=False
    )
```
